256 devices in a mesh: ta: 8 (over x, core), xyz: 32 (over y, z).
Axes of the slice: x: 4, y: 4, z: 8, core: 2. Of those that a mesh axis runs over, the one named last changes fastest.
Arguments:
- nulls: bfloat16 [32, 128, 32, 16, 128], P('ta', 'xyz'), may hold values from -1.1953125 to 1.1953125
- time_links: bfloat16 [16, 128, 32, 64, 128], P('ta', 'xyz'), may hold values from -0.5 to 0.5
- space_links: bfloat16 [32, 64, 32, 64, 128], P('ta', 'xyz'), may hold values from -0.5 to 0.5
- owner_lists: int32 [32, 64], replicated, may hold values from -1 to 1023, as said below
Outputs:
- coarse_links: float32 [8, 2048, 1024], P('ta', 'xyz')
The draws below stay inside these ranges and needn't reach their ends.
Inputs may be any that keep to these rules, and one draw needn't show every extreme that they name: `owner_lists`: row d lists, in increasing order, the aggregates that shard d owns, followed by -1 in the remaining slots; each of the 1024 aggregate ids appears exactly once. Exactly half of the shards own 64 aggregates each and the others none. The 32 aggregates with ids q * 32 to q * 32 + 31 belong to exactly 8 owners, 4 to each.
All inputs are finite; a program needn't handle non-finite values.
Results may differ from the reference program's by a relative error of at most 0.0029.
Values may be sent and summed in bfloat16 or wider, within the bound.
A program may use at most 64 MiB of HBM per device.

```python
import jax
import jax.numpy as jnp
from jax import lax

FINE = 64
NV = 16
AT = 2
AX = 2
AS = 8
A_DEV = 32
LT = 32
LX = 128
YZ = 32
SEND_MOST = 4
CAP = 64
N_TA = 8
N_XYZ = 32


def draw_owner_lists(key, part):
    heavy_key = jax.random.fold_in(key, 11)
    order_key = jax.random.fold_in(key, 12)
    half_count = N_XYZ // 2
    heavy = jax.random.permutation(heavy_key, N_XYZ)[:half_count]
    shard_keys = jax.random.split(order_key, N_XYZ)
    orders = jax.vmap(lambda shard_key: jax.random.permutation(shard_key, A_DEV))(shard_keys)
    places = jnp.argsort(orders, axis=1)
    groups_of = places // SEND_MOST
    shard_ids = jnp.arange(N_XYZ)[:, None]
    owners = heavy[(shard_ids + groups_of) % half_count].reshape(-1)
    agg_ids = (shard_ids * A_DEV + jnp.arange(A_DEV)[None, :]).reshape(-1)
    beyond = N_XYZ * A_DEV
    keyed = jnp.where(owners[None, :] == jnp.arange(N_XYZ)[:, None], agg_ids[None, :], beyond)
    ordered = jnp.sort(keyed, axis=1)[:, :CAP]
    return jnp.where(ordered == beyond, -1, ordered).astype(jnp.int32)


def level_of(key, extent, shards, smallest, top_value):
    def one(dim, parts):
        steps = jax.random.uniform(jax.random.fold_in(jax.random.fold_in(key, 6), dim), (parts,), jnp.float32, smallest / len(shards), top_value / len(shards))
        return jnp.repeat(jnp.exp(steps), extent[dim] // parts).reshape((-1,) + (1,) * (len(extent) - dim - 1))

    gain = one(*shards[0])
    for cut in shards[1:]:
        gain = gain * one(*cut)
    return gain


def centred(own_key, shape, deviation, bound, shards=(), kind=jnp.bfloat16):
    result = jax.random.normal(own_key, shape, jnp.float32) * deviation
    if len(shards) > 0:
        result = level_of(own_key, shape, shards, -0.22, 0.18) * result
    return jnp.clip(result, min=-bound, max=bound).astype(kind)


def setup_inputs(seed: int = 0) -> dict:
    keys = jax.random.split(jax.random.key(seed), 5)
    nulls = centred(keys[0], (LT, LX, YZ, NV, 2 * FINE), 0.2, 1.1953125, ((0, 8), (1, 32)))
    time_links = centred(keys[1], (LT // 2, LX, YZ, FINE, 2 * FINE), (2 * FINE) ** -0.5, 0.5, ((0, 8), (1, 32)))
    space_links = centred(keys[2], (LT, LX // 2, YZ, FINE, 2 * FINE), (2 * FINE) ** -0.5, 0.5, ((0, 8), (1, 32)))
    owner_lists = draw_owner_lists(jax.random.fold_in(keys[4], 71), 0)
    return dict(nulls=nulls, time_links=time_links, space_links=space_links, owner_lists=owner_lists)


def forward_image(link_mats, upper_nulls):
    half_width = link_mats.shape[-2]
    upper_real = upper_nulls[..., :half_width]
    upper_imag = upper_nulls[..., half_width:]
    paired = jnp.stack([jnp.concatenate([upper_real, -upper_imag], axis=-1), jnp.concatenate([upper_imag, upper_real], axis=-1)], axis=-3)
    image_pair = jnp.einsum("...ik,...pnk->...pni", link_mats.astype(jnp.float32), paired.astype(jnp.float32), precision=lax.Precision.HIGHEST)
    joined = jnp.concatenate([image_pair[..., 0, :, :], image_pair[..., 1, :, :]], axis=-1)
    return joined.astype(jnp.bfloat16)


def conjugate_pair(lower_nulls):
    half_width = lower_nulls.shape[-1] // 2
    turned = jnp.concatenate([-lower_nulls[..., half_width:], lower_nulls[..., :half_width]], axis=-1)
    return jnp.stack([lower_nulls, turned], axis=-3)


def reference(nulls, time_links, space_links, owner_lists):
    time_sites = nulls.shape[0]
    half_time = time_sites // 2
    time_lower = nulls[1::2]
    time_upper = jnp.roll(nulls, -1, axis=0)[1::2]
    space_lower = nulls[:, 1::2]
    space_upper = jnp.roll(nulls, -1, axis=1)[:, 1::2]

    def regroup(array):
        return array.reshape((half_time, 2) + array.shape[1:])

    def one_step(step_items):
        time_mats, low_time, up_time, space_mats, low_space, up_space = step_items
        x_sites = time_mats.shape[0]
        w_sites = time_mats.shape[1]
        vectors = low_time.shape[-2]
        doubled = low_time.shape[-1]
        image_time = forward_image(time_mats, up_time).astype(jnp.float32).reshape(x_sites // 2, 2, w_sites // 4, 4, vectors, doubled)
        pair_time = conjugate_pair(low_time).astype(jnp.float32).reshape(x_sites // 2, 2, w_sites // 4, 4, 2, vectors, doubled)
        block_time = jnp.einsum("xcaypnk,xcaymk->xapnm", pair_time, image_time, precision=lax.Precision.HIGHEST)
        image_space = forward_image(space_mats, up_space).astype(jnp.float32).reshape(2, x_sites // 2, w_sites // 4, 4, vectors, doubled)
        pair_space = conjugate_pair(low_space).astype(jnp.float32).reshape(2, x_sites // 2, w_sites // 4, 4, 2, vectors, doubled)
        block_space = jnp.einsum("cxaypnk,cxaymk->xapnm", pair_space, image_space, precision=lax.Precision.HIGHEST)
        block_width = 2 * vectors * vectors
        return jnp.concatenate([block_time.reshape(x_sites // 2, w_sites // 4, block_width), block_space.reshape(x_sites // 2, w_sites // 4, block_width)], axis=-1)

    all_rows = lax.map(one_step, (time_links, time_lower, time_upper, regroup(space_links), regroup(space_lower), regroup(space_upper)))
    row_len = all_rows.shape[-1]
    grouped = all_rows.reshape(N_TA, AT, N_XYZ, AX, AS, row_len).transpose(0, 2, 1, 3, 4, 5).reshape(N_TA, N_XYZ * AT * AX * AS, row_len)
    flat_lists = owner_lists.reshape(-1).astype(jnp.int32)
    live_slot = (flat_lists >= 0).astype(jnp.float32)
    picked = jnp.take(grouped, jnp.maximum(flat_lists, 0), axis=1)
    return picked * live_slot[None, :, None]
```

```python
import functools

import jax
import jax.numpy as jnp
from jax import lax
from jax.experimental import pallas as pl
from jax.experimental.pallas import tpu as pltpu
from jax.sharding import PartitionSpec as P

MESH = pl.DeviceIdType.MESH
NY, NZ = 4, 8
BF, F32, I32 = jnp.bfloat16, jnp.float32, jnp.int32


def dot_nt(a, b):
    return lax.dot_general(a, b, (((1,), (1,)), ((), ())), preferred_element_type=F32)


def dot_nn(a, b):
    return lax.dot_general(a, b, (((1,), (0,)), ((), ())), preferred_element_type=F32)


def iota(shape, dim):
    return lax.broadcasted_iota(I32, shape, dim)


def one_hot(cond):
    return jnp.where(cond, 1.0, 0.0).astype(BF)


def swap_halves(x):
    return jnp.concatenate([x[:, 64:], x[:, :64]], axis=1)


def kernel(
    nulls_hbm, tl_hbm, sl_hbm, owner_ref, out_ref,
    nulls, tl, sl, th, sh, zm, group_rows, pack, unpack, send, recv,
    nulls_sem, link_sem, halo_send, halo_recv, row_send, row_recv, own_sem,
):
    ta = lax.axis_index("ta")
    me = lax.axis_index("xyz")
    n_ta, n_xyz = 8, NY * NZ
    my_y, my_z = me // NZ, me % NZ
    ta_down, ta_up = (ta + n_ta - 1) % n_ta, (ta + 1) % n_ta
    down = (me + n_xyz - 1) % n_xyz

    def peer(k):
        kz, ky = k // NY, k % NY
        half = kz // 2 + kz % 2
        dz = jnp.where(kz == 7, 0, jnp.where(kz % 2 == 1, 4 + half, 4 - half))
        dy = jnp.where(ky == 3, 0, jnp.where(ky % 2 == 1, 3, 2 - ky // 2))
        return ((my_y + dy) % NY) * NZ + (my_z + dz) % NZ

    barrier = pltpu.get_barrier_semaphore()
    pl.semaphore_signal(barrier, inc=1, device_id={"ta": ta_down}, device_id_type=MESH)
    pl.semaphore_signal(barrier, inc=1, device_id={"ta": ta_up}, device_id_type=MESH)

    @pl.loop(0, n_xyz - 1)
    def _(k):
        pl.semaphore_signal(barrier, inc=1, device_id={"xyz": peer(k)}, device_id_type=MESH)

    nulls_copy = pltpu.make_async_copy(nulls_hbm, nulls, nulls_sem)
    nulls_copy.start()
    groups = [("t", 0, 0), ("t", 0, 1), ("s", 0, 0), ("s", 1, 0), ("t", 1, 0), ("t", 1, 1), ("s", 0, 1), ("s", 1, 1)]
    link_copies = {}
    for i, (kind, at, ax) in enumerate(groups):
        if kind == "t":
            src, dst = tl_hbm.at[at, pl.ds(2 * ax, 2)], tl.at[at, pl.ds(2 * ax, 2)]
        else:
            src, dst = sl_hbm.at[pl.ds(2 * at, 2), ax], sl.at[pl.ds(2 * at, 2), ax]
        link_copies[kind, at, ax] = pltpu.make_async_copy(src, dst, link_sem.at[i])
        link_copies[kind, at, ax].start()

    pl.semaphore_wait(barrier, n_xyz + 1)

    halo = {}
    for part in range(2):
        halo["s", part] = pltpu.make_async_remote_copy(
            nulls_hbm.at[pl.ds(2 * part, 2), 0], sh.at[pl.ds(2 * part, 2)],
            halo_send.at[2 + part], halo_recv.at[2 + part], device_id={"xyz": down}, device_id_type=MESH)
        halo["t", part] = pltpu.make_async_remote_copy(
            nulls_hbm.at[0, pl.ds(2 * part, 2)], th.at[pl.ds(2 * part, 2)],
            halo_send.at[part], halo_recv.at[part], device_id={"ta": ta_down}, device_id_type=MESH)
        halo["s", part].start()
        halo["t", part].start()

    row, col = iota((128, 1024), 0), iota((128, 1024), 1)
    group_rows[...] = one_hot(((row % 32) == (col // 32)) & ((row // 32) == ((col // 8) % 4)))
    lists = owner_ref[...]
    wide = jnp.broadcast_to(lists[:, None, :], (32, 16, 64)).reshape(512, 64)
    base = me * 32
    first = jnp.sum(jnp.where((wide >= 0) & (wide < base), 1, 0), axis=1, keepdims=True)
    r512 = iota((512, 1), 0)
    agg = jnp.sum(jnp.where(iota((512, 64), 1) == first + r512 % 4, wide, 0), axis=1, keepdims=True) - base
    target = jnp.where((agg >= 0) & (agg < 32), ((r512 // 4) % 4) * 32 + agg, -1)
    pack[...] = one_hot(iota((512, 128), 1) == target)
    mine = jnp.broadcast_to(owner_ref[pl.ds(me, 1), :], (256, 64))
    r256 = iota((256, 1), 0)
    slot = r256 % 64
    listed = jnp.sum(jnp.where(iota((256, 64), 1) == slot, mine, 0), axis=1, keepdims=True)
    place = jnp.where(listed >= 0, (listed // 32) * 16 + (r256 // 64) * 4 + slot % 4, -1)
    unpack[...] = one_hot(iota((256, 512), 1) == place)

    lane = iota((16, 128), 1)
    low16 = lane < 64
    low32 = iota((32, 128), 1) < 64
    spread = one_hot(iota((16, 128), 0) == iota((16, 128), 1) % 16)
    keep = (iota((32, 128), 1) // 16) == (iota((32, 128), 0) % 8)

    def aggregate(half, agg, links, uppers, lowers):
        left, right = [], []
        for c in range(2):
            for w in range(0, 4, 2):
                a, b = uppers(c, w), uppers(c, w + 1)
                sa, sb = jnp.where(low16, a, -a), jnp.where(low16, b, -b)
                paired = jnp.concatenate([sa, swap_halves(a), sb, swap_halves(b)], axis=0)
                product = dot_nt(paired, links(c, w))
                image = jnp.where(low32, product[:32], product[32:]).astype(BF)
                right.append(image[:16])
                right.append(image[16:])
                la, lb = lowers(c, w), lowers(c, w + 1)
                re = jnp.where(low16, la, swap_halves(lb))
                im = jnp.where(low16, swap_halves(la), lb)
                left.append(jnp.concatenate([re, -im], axis=0))
                left.append(jnp.concatenate([im, re], axis=0))
        block = dot_nt(jnp.concatenate(left, axis=1), jnp.concatenate(right, axis=1))
        tiled = dot_nn(block.astype(BF), spread)
        zm[half, pl.ds(agg * 32, 32), :] = jnp.where(keep, tiled, 0.0).astype(BF)

    def group(kind, at, ax):
        link_copies[kind, at, ax].wait()

        def body(aw, _):
            w0 = aw * 4
            if kind == "t":
                def links(c, w):
                    return tl[at, 2 * ax + c, pl.ds(w0 + w, 2)].reshape(128, 128)

                def uppers(c, w):
                    return nulls[2, 2 * ax + c, w0 + w] if at == 0 else th[2 * ax + c, w0 + w]

                def lowers(c, w):
                    return nulls[2 * at + 1, 2 * ax + c, w0 + w]
            else:
                def links(c, w):
                    return sl[2 * at + c, ax, pl.ds(w0 + w, 2)].reshape(128, 128)

                def uppers(c, w):
                    return nulls[2 * at + c, 2, w0 + w] if ax == 0 else sh[2 * at + c, w0 + w]

                def lowers(c, w):
                    return nulls[2 * at + c, 2 * ax + 1, w0 + w]
            aggregate(0 if kind == "t" else 1, (at * 2 + ax) * 8 + aw, links, uppers, lowers)
            return 0

        lax.fori_loop(0, 8, body, 0, unroll=2)

    def row_copy(half, to, slot):
        return pltpu.make_async_remote_copy(
            send.at[half, to], recv.at[half, me], row_send.at[half, to], row_recv.at[half, slot],
            device_id={"xyz": to}, device_id_type=MESH)

    def deliver(half):
        rows = dot_nn(group_rows[...], zm[half]).astype(BF)
        send[half] = dot_nn(pack[...], rows).astype(BF).reshape(n_xyz, 16, 128)

        @pl.loop(0, n_xyz - 1)
        def _(k):
            row_copy(half, peer(k), me).start()

        pltpu.make_async_copy(send.at[half, me], recv.at[half, me], own_sem.at[half]).start()

    def collect(half):
        pltpu.make_async_copy(send.at[half, me], recv.at[half, me], own_sem.at[half]).wait()

        @pl.loop(0, n_xyz - 1)
        def _(k):
            to = peer(k)
            row_copy(half, to, to).wait()

        placed = dot_nn(unpack[...], recv[half].reshape(512, 128))
        for q in range(4):
            out_ref[:, half * 512 + q * 128:half * 512 + (q + 1) * 128] = placed[q * 64:(q + 1) * 64]

    nulls_copy.wait()
    group("t", 0, 0)
    group("t", 0, 1)
    group("s", 0, 0)
    group("s", 1, 0)
    halo["t", 0].wait()
    group("t", 1, 0)
    halo["t", 1].wait()
    group("t", 1, 1)
    deliver(0)
    halo["s", 0].wait()
    group("s", 0, 1)
    halo["s", 1].wait()
    group("s", 1, 1)
    deliver(1)
    collect(0)
    collect(1)


def on_device(nulls, time_links, space_links, owner_lists):
    result = pl.pallas_call(
        kernel,
        out_shape=jax.ShapeDtypeStruct((64, 1024), F32),
        in_specs=[pl.BlockSpec(memory_space=pl.ANY)] * 3 + [pl.BlockSpec(memory_space=pltpu.VMEM)],
        out_specs=pl.BlockSpec(memory_space=pltpu.VMEM),
        scratch_shapes=[
            pltpu.VMEM((4, 4, 32, 16, 128), BF),
            pltpu.VMEM((2, 4, 32, 64, 128), BF),
            pltpu.VMEM((4, 2, 32, 64, 128), BF),
            pltpu.VMEM((4, 32, 16, 128), BF),
            pltpu.VMEM((4, 32, 16, 128), BF),
            pltpu.VMEM((2, 1024, 128), BF),
            pltpu.VMEM((128, 1024), BF),
            pltpu.VMEM((512, 128), BF),
            pltpu.VMEM((256, 512), BF),
            pltpu.VMEM((2, 32, 16, 128), BF),
            pltpu.VMEM((2, 32, 16, 128), BF),
            pltpu.SemaphoreType.DMA,
            pltpu.SemaphoreType.DMA((8,)),
            pltpu.SemaphoreType.DMA((4,)),
            pltpu.SemaphoreType.DMA((4,)),
            pltpu.SemaphoreType.DMA((2, 32)),
            pltpu.SemaphoreType.DMA((2, 32)),
            pltpu.SemaphoreType.DMA((2,)),
        ],
        compiler_params=pltpu.CompilerParams(collective_id=0, has_side_effects=True),
    )(nulls, time_links, space_links, owner_lists)
    return result[None]


def solution(mesh):
    return jax.shard_map(
        on_device,
        mesh=mesh,
        in_specs=(
            P("ta", "xyz", None, None, None),
            P("ta", "xyz", None, None, None),
            P("ta", "xyz", None, None, None),
            P(),
        ),
        out_specs=P("ta", "xyz", None),
        check_vma=False,
    )
```

```python
import functools

import jax
import jax.numpy as jnp
from jax import lax
from jax.experimental import pallas as pl
from jax.experimental.pallas import tpu as pltpu
from jax.sharding import PartitionSpec as P

MESH = pl.DeviceIdType.MESH
NY, NZ = 4, 8
BF, F32, I32 = jnp.bfloat16, jnp.float32, jnp.int32


def dot_nt(a, b):
    return lax.dot_general(a, b, (((1,), (1,)), ((), ())), preferred_element_type=F32)


def dot_nn(a, b):
    return lax.dot_general(a, b, (((1,), (0,)), ((), ())), preferred_element_type=F32)


def iota(shape, dim):
    return lax.broadcasted_iota(I32, shape, dim)


def one_hot(cond):
    return jnp.where(cond, 1.0, 0.0).astype(BF)


def swap_halves(x):
    return jnp.concatenate([x[:, 64:], x[:, :64]], axis=1)


def kernel(
    nulls_hbm, tl_hbm, sl_hbm, owner_ref, out_ref,
    nulls, tl, sl, th, sh, held, row_parts, group_rows, pack, unpack, send, recv,
    nulls_sem, link_sem, halo_send, halo_recv, row_send, row_recv, own_sem,
):
    ta = lax.axis_index("ta")
    me = lax.axis_index("xyz")
    n_ta, n_xyz = 8, NY * NZ
    my_y, my_z = me // NZ, me % NZ
    ta_down, ta_up = (ta + n_ta - 1) % n_ta, (ta + 1) % n_ta
    down = (me + n_xyz - 1) % n_xyz

    def peer(k):
        kz, ky = k // NY, k % NY
        half = kz // 2 + kz % 2
        dz = jnp.where(kz == 7, 0, jnp.where(kz % 2 == 1, 4 + half, 4 - half))
        dy = jnp.where(ky == 3, 0, jnp.where(ky % 2 == 1, 3, 2 - ky // 2))
        return ((my_y + dy) % NY) * NZ + (my_z + dz) % NZ

    barrier = pltpu.get_barrier_semaphore()
    pl.semaphore_signal(barrier, inc=1, device_id={"ta": ta_down}, device_id_type=MESH)
    pl.semaphore_signal(barrier, inc=1, device_id={"ta": ta_up}, device_id_type=MESH)

    @pl.loop(0, n_xyz - 1)
    def _(k):
        pl.semaphore_signal(barrier, inc=1, device_id={"xyz": peer(k)}, device_id_type=MESH)

    nulls_copy = pltpu.make_async_copy(nulls_hbm, nulls, nulls_sem)
    nulls_copy.start()
    groups = [("t", 0, 0), ("t", 0, 1), ("s", 0, 0), ("s", 1, 0), ("t", 1, 0), ("t", 1, 1), ("s", 0, 1), ("s", 1, 1)]
    link_copies = {}
    for i, (kind, at, ax) in enumerate(groups):
        if kind == "t":
            src, dst = tl_hbm.at[at, pl.ds(2 * ax, 2)], tl.at[at, pl.ds(2 * ax, 2)]
        else:
            src, dst = sl_hbm.at[pl.ds(2 * at, 2), ax], sl.at[pl.ds(2 * at, 2), ax]
        link_copies[kind, at, ax] = pltpu.make_async_copy(src, dst, link_sem.at[i])
        link_copies[kind, at, ax].start()

    pl.semaphore_wait(barrier, n_xyz + 1)

    halo = {}
    for part in range(2):
        halo["s", part] = pltpu.make_async_remote_copy(
            nulls_hbm.at[pl.ds(2 * part, 2), 0], sh.at[pl.ds(2 * part, 2)],
            halo_send.at[2 + part], halo_recv.at[2 + part], device_id={"xyz": down}, device_id_type=MESH)
        halo["t", part] = pltpu.make_async_remote_copy(
            nulls_hbm.at[0, pl.ds(2 * part, 2)], th.at[pl.ds(2 * part, 2)],
            halo_send.at[part], halo_recv.at[part], device_id={"ta": ta_down}, device_id_type=MESH)
        halo["s", part].start()
        halo["t", part].start()

    row, col = iota((32, 256), 0), iota((32, 256), 1)
    group_rows[...] = one_hot(((row % 8) == (col // 32)) & ((row // 8) == ((col // 8) % 4)))
    lists = owner_ref[...]
    wide = jnp.broadcast_to(lists[:, None, :], (32, 16, 64)).reshape(512, 64)
    base = me * 32
    first = jnp.sum(jnp.where((wide >= 0) & (wide < base), 1, 0), axis=1, keepdims=True)
    r512 = iota((512, 1), 0)
    agg = jnp.sum(jnp.where(iota((512, 64), 1) == first + r512 % 4, wide, 0), axis=1, keepdims=True) - base
    target = jnp.where((agg >= 0) & (agg < 32), ((r512 // 4) % 4) * 32 + agg, -1)
    pack[...] = one_hot(iota((512, 128), 1) == target)
    mine = jnp.broadcast_to(owner_ref[pl.ds(me, 1), :], (256, 64))
    r256 = iota((256, 1), 0)
    slot = r256 % 64
    listed = jnp.sum(jnp.where(iota((256, 64), 1) == slot, mine, 0), axis=1, keepdims=True)
    place = jnp.where(listed >= 0, (listed // 32) * 16 + (r256 // 64) * 4 + slot % 4, -1)
    unpack[...] = one_hot(iota((256, 512), 1) == place)

    low16 = iota((16, 128), 1) < 64
    low32 = iota((32, 128), 1) < 64
    turn = jnp.where(low16, 1.0, -1.0).astype(BF)
    spread = one_hot(iota((16, 128), 0) == iota((16, 128), 1) % 16)
    keep = (iota((256, 128), 1) // 16) == (iota((256, 128), 0) % 8)
    none = jnp.zeros((32, 128), BF)

    def images(c, w, links, uppers):
        mats = links(c, w)
        weights = jnp.concatenate(
            [jnp.concatenate([mats[0], mats[2]], axis=0), jnp.concatenate([mats[1], mats[3]], axis=0)], axis=1)
        rows = []
        for i in range(4):
            v = uppers(c, w + i)
            paired = jnp.concatenate([v * turn, swap_halves(v)], axis=0)
            rows.append(jnp.concatenate([none, paired] if i % 2 else [paired, none], axis=1))
        product = dot_nt(jnp.concatenate(rows, axis=0), weights)
        for i in range(2):
            yield jnp.where(low32, product[32 * i:32 * i + 32], product[64 + 32 * i:96 + 32 * i]).astype(BF)

    def conjugates(c, w, lowers):
        for i in range(2):
            a, b = lowers(c, w + i), lowers(c, w + i + 2)
            re = jnp.where(low16, a, swap_halves(b))
            im = jnp.where(low16, swap_halves(a), b)
            yield jnp.concatenate([re, -im], axis=0)
            yield jnp.concatenate([im, re], axis=0)

    def group(kind, at, ax):
        if kind == "t":
            def links(c, w):
                return [tl[at, 2 * ax + c, w + i] for i in range(4)]

            def uppers(c, w):
                return nulls[2, 2 * ax + c, w] if at == 0 else th[2 * ax + c, w]

            def lowers(c, w):
                return nulls[2 * at + 1, 2 * ax + c, w]
        else:
            def links(c, w):
                return [sl[2 * at + c, ax, w + i] for i in range(4)]

            def uppers(c, w):
                return nulls[2 * at + c, 2, w] if ax == 0 else sh[2 * at + c, w]

            def lowers(c, w):
                return nulls[2 * at + c, 2 * ax + 1, w]
        slot = (at * 2 + ax) + (0 if kind == "t" else 4)
        for aw in range(8):
            for c in range(2):
                for i, image in enumerate(images(c, 4 * aw, links, uppers)):
                    k = (c * 2 + i) * 256
                    held[slot, aw, :, k:k + 128] = image[:16]
                    held[slot, aw, :, k + 128:k + 256] = image[16:]
        blocks = []
        for aw in range(8):
            left = jnp.concatenate([x for c in range(2) for x in conjugates(c, 4 * aw, lowers)], axis=1)
            blocks.append(dot_nt(left, held[slot, aw]))
        tiled = dot_nn(jnp.concatenate(blocks, axis=0).astype(BF), spread)
        rows = dot_nn(group_rows[...], jnp.where(keep, tiled, 0.0).astype(BF))
        half = 0 if kind == "t" else 1
        for q in range(4):
            row_parts[half, pl.ds(q * 32 + (at * 2 + ax) * 8, 8), :] = rows[8 * q:8 * q + 8]

    def row_copy(half, to, slot):
        return pltpu.make_async_remote_copy(
            send.at[half, to], recv.at[half, me], row_send.at[half, to], row_recv.at[half, slot],
            device_id={"xyz": to}, device_id_type=MESH)

    def deliver(half):
        send[half] = dot_nn(pack[...], row_parts[half].astype(BF)).astype(BF).reshape(n_xyz, 16, 128)

        @pl.loop(0, n_xyz - 1)
        def _(k):
            row_copy(half, peer(k), me).start()

        pltpu.make_async_copy(send.at[half, me], recv.at[half, me], own_sem.at[half]).start()

    def collect(half):
        pltpu.make_async_copy(send.at[half, me], recv.at[half, me], own_sem.at[half]).wait()

        @pl.loop(0, n_xyz - 1)
        def _(k):
            to = peer(k)
            row_copy(half, to, to).wait()

        placed = dot_nn(unpack[...], recv[half].reshape(512, 128))
        for q in range(4):
            out_ref[:, half * 512 + q * 128:half * 512 + (q + 1) * 128] = placed[q * 64:(q + 1) * 64]

    nulls_copy.wait()
    for key in groups:
        link_copies[key].wait()
    group("t", 0, 0)
    group("t", 0, 1)
    group("s", 0, 0)
    group("s", 1, 0)
    halo["t", 0].wait()
    group("t", 1, 0)
    halo["t", 1].wait()
    group("t", 1, 1)
    deliver(0)
    halo["s", 0].wait()
    group("s", 0, 1)
    halo["s", 1].wait()
    group("s", 1, 1)
    deliver(1)
    collect(0)
    collect(1)


def on_device(nulls, time_links, space_links, owner_lists):
    result = pl.pallas_call(
        kernel,
        out_shape=jax.ShapeDtypeStruct((64, 1024), F32),
        in_specs=[pl.BlockSpec(memory_space=pl.ANY)] * 3 + [pl.BlockSpec(memory_space=pltpu.VMEM)],
        out_specs=pl.BlockSpec(memory_space=pltpu.VMEM),
        scratch_shapes=[
            pltpu.VMEM((4, 4, 32, 16, 128), BF),
            pltpu.VMEM((2, 4, 32, 64, 128), BF),
            pltpu.VMEM((4, 2, 32, 64, 128), BF),
            pltpu.VMEM((4, 32, 16, 128), BF),
            pltpu.VMEM((4, 32, 16, 128), BF),
            pltpu.VMEM((8, 8, 16, 1024), BF),
            pltpu.VMEM((2, 128, 128), F32),
            pltpu.VMEM((32, 256), BF),
            pltpu.VMEM((512, 128), BF),
            pltpu.VMEM((256, 512), BF),
            pltpu.VMEM((2, 32, 16, 128), BF),
            pltpu.VMEM((2, 32, 16, 128), BF),
            pltpu.SemaphoreType.DMA,
            pltpu.SemaphoreType.DMA((8,)),
            pltpu.SemaphoreType.DMA((4,)),
            pltpu.SemaphoreType.DMA((4,)),
            pltpu.SemaphoreType.DMA((2, 32)),
            pltpu.SemaphoreType.DMA((2, 32)),
            pltpu.SemaphoreType.DMA((2,)),
        ],
        compiler_params=pltpu.CompilerParams(collective_id=0, has_side_effects=True),
    )(nulls, time_links, space_links, owner_lists)
    return result[None]


def solution(mesh):
    return jax.shard_map(
        on_device,
        mesh=mesh,
        in_specs=(
            P("ta", "xyz", None, None, None),
            P("ta", "xyz", None, None, None),
            P("ta", "xyz", None, None, None),
            P(),
        ),
        out_specs=P("ta", "xyz", None),
        check_vma=False,
    )
```

```python
import functools

import jax
import jax.numpy as jnp
from jax import lax
from jax.experimental import pallas as pl
from jax.experimental.pallas import tpu as pltpu
from jax.sharding import PartitionSpec as P

MESH = pl.DeviceIdType.MESH
NY, NZ = 4, 8
BF, F32, I32 = jnp.bfloat16, jnp.float32, jnp.int32


def dot_nt(a, b):
    return lax.dot_general(a, b, (((1,), (1,)), ((), ())), preferred_element_type=F32)


def dot_nn(a, b):
    return lax.dot_general(a, b, (((1,), (0,)), ((), ())), preferred_element_type=F32)


def iota(shape, dim):
    return lax.broadcasted_iota(I32, shape, dim)


def one_hot(cond):
    return jnp.where(cond, 1.0, 0.0).astype(BF)


def swap_halves(x):
    return jnp.concatenate([x[:, 64:], x[:, :64]], axis=1)


def kernel(
    nulls_hbm, tl_hbm, sl_hbm, owner_ref, out_ref,
    nulls, tl, sl, th, sh, held, row_parts, through, back, group_rows, pack, unpack, send, recv,
    nulls_sem, link_sem, halo_send, halo_recv, row_send, row_recv, own_sem,
):
    ta = lax.axis_index("ta")
    me = lax.axis_index("xyz")
    n_ta, n_xyz = 8, NY * NZ
    ta_down, ta_up = lax.rem(ta + n_ta - 1, n_ta), lax.rem(ta + 1, n_ta)
    down, up = lax.rem(me + n_xyz - 1, n_xyz), lax.rem(me + 1, n_xyz)
    my_y, my_z = lax.div(me, NZ), lax.rem(me, NZ)
    rows_y = [lax.rem(my_y + dy, NY) * NZ for dy in range(NY)]
    rows_z = [lax.rem(my_z + dz, NZ) for dz in range(NZ)]
    peers = [rows_y[dy] + rows_z[dz] for dz in (4, 3, 5, 2, 6, 1, 7, 0) for dy in (2, 1, 3, 0)][:-1]

    barrier = pltpu.get_barrier_semaphore()
    pl.semaphore_signal(barrier, inc=1, device_id={"ta": ta_down}, device_id_type=MESH)
    pl.semaphore_signal(barrier, inc=1, device_id={"ta": ta_up}, device_id_type=MESH)

    for peer in peers:
        pl.semaphore_signal(barrier, inc=1, device_id={"xyz": peer}, device_id_type=MESH)

    nulls_copy = pltpu.make_async_copy(nulls_hbm, nulls, nulls_sem)
    nulls_copy.start()
    groups = [("s", 1, 1), ("t", 0, 0), ("t", 0, 1), ("s", 0, 0), ("s", 1, 0), ("t", 1, 0), ("t", 1, 1), ("s", 0, 1)]
    link_copies = {}
    for i, (kind, at, ax) in enumerate(groups):
        if kind == "t":
            src, dst = tl_hbm.at[at, pl.ds(2 * ax, 2)], tl.at[at, pl.ds(2 * ax, 2)]
        else:
            src, dst = sl_hbm.at[pl.ds(2 * at, 2), ax], sl.at[pl.ds(2 * at, 2), ax]
        link_copies[kind, at, ax] = pltpu.make_async_copy(src, dst, link_sem.at[i])
        link_copies[kind, at, ax].start()

    row, col = iota((32, 256), 0), iota((32, 256), 1)
    group_rows[...] = one_hot(((row % 8) == (col // 32)) & ((row // 8) == ((col // 8) % 4)))
    lists = owner_ref[...]
    wide = jnp.broadcast_to(lists[:, None, :], (32, 16, 64)).reshape(512, 64)
    base = me * 32
    first = jnp.sum(jnp.where((wide >= 0) & (wide < base), 1, 0), axis=1, keepdims=True)
    r512 = iota((512, 1), 0)
    agg = jnp.sum(jnp.where(iota((512, 64), 1) == first + r512 % 4, wide, 0), axis=1, keepdims=True) - base
    target = jnp.where((agg >= 0) & (agg < 32), ((r512 // 4) % 4) * 32 + agg, -1)
    pack[...] = one_hot(iota((512, 128), 1) == target)
    mine = jnp.broadcast_to(owner_ref[pl.ds(me, 1), :], (256, 64))
    r256 = iota((256, 1), 0)
    slot = r256 % 64
    listed = jnp.sum(jnp.where(iota((256, 64), 1) == slot, mine, 0), axis=1, keepdims=True)
    place = jnp.where(listed >= 0, (listed // 32) * 16 + (r256 // 64) * 4 + slot % 4, -1)
    unpack[...] = one_hot(iota((256, 512), 1) == place)

    low16 = iota((16, 128), 1) < 64
    low32 = iota((32, 128), 1) < 64
    turn = jnp.where(low16, 1.0, -1.0).astype(BF)
    spread = one_hot(iota((16, 128), 0) == iota((16, 128), 1) % 16)
    keep = (iota((256, 128), 1) // 16) == (iota((256, 128), 0) % 8)
    none = jnp.zeros((32, 128), BF)

    def images(c, w, links, uppers):
        mats = links(c, w)
        weights = jnp.concatenate(
            [jnp.concatenate([mats[0], mats[2]], axis=0), jnp.concatenate([mats[1], mats[3]], axis=0)], axis=1)
        rows = []
        for i in range(4):
            v = uppers(c, w + i)
            paired = jnp.concatenate([v * turn, swap_halves(v)], axis=0)
            rows.append(jnp.concatenate([none, paired] if i % 2 else [paired, none], axis=1))
        product = dot_nt(jnp.concatenate(rows, axis=0), weights)
        for i in range(2):
            yield jnp.where(low32, product[32 * i:32 * i + 32], product[64 + 32 * i:96 + 32 * i]).astype(BF)

    def conjugates(c, w, lowers):
        for i in range(2):
            a, b = lowers(c, w + i), lowers(c, w + i + 2)
            re = jnp.where(low16, a, swap_halves(b))
            im = jnp.where(low16, swap_halves(a), b)
            yield jnp.concatenate([re, -im], axis=0)
            yield jnp.concatenate([im, re], axis=0)

    def merge(blocks):
        tiled = dot_nn(jnp.concatenate(blocks, axis=0).astype(BF), spread)
        return dot_nn(group_rows[...], jnp.where(keep, tiled, 0.0).astype(BF))

    def place(half, part, rows):
        for q in range(4):
            row_parts[half, pl.ds(q * 32 + part * 8, 8), :] = rows[8 * q:8 * q + 8]

    def conjugate_through():
        zero = jnp.zeros((16, 128), BF)
        for c in range(2):
            for w in range(0, 32, 4):
                rows = []
                for i in range(4):
                    v = nulls[2 + c, 3, w + i]
                    t = swap_halves(v)
                    if i % 2 == 0:
                        part = jnp.concatenate([jnp.where(low16, v, zero), jnp.where(low16, t, zero)], axis=0)
                    else:
                        part = jnp.concatenate([jnp.where(low16, zero, t), jnp.where(low16, zero, v)], axis=0)
                    rows.append(jnp.concatenate([part, none] if i < 2 else [none, part], axis=1))
                weights = jnp.concatenate([sl[2 + c, 1, w + i] for i in range(4)], axis=0)
                product = dot_nn(jnp.concatenate(rows, axis=0), weights)
                for i in range(4):
                    top, low = product[32 * i:32 * i + 16], product[32 * i + 16:32 * i + 32]
                    through[0, c, w + i] = (top + jnp.where(low16, swap_halves(low), -swap_halves(low))).astype(BF)

    def blocks_through(aw):
        left, right = [], []
        for c in range(2):
            for w in range(4 * aw, 4 * aw + 4):
                v = through[1, c, w]
                left.append(jnp.concatenate([v * turn, swap_halves(v)], axis=0))
                right.append(nulls[2 + c, 0, w])
        return dot_nt(jnp.concatenate(left, axis=1), jnp.concatenate(right, axis=1))

    def group(kind, at, ax):
        if kind == "t":
            def links(c, w):
                return [tl[at, 2 * ax + c, w + i] for i in range(4)]

            def uppers(c, w):
                return nulls[2, 2 * ax + c, w] if at == 0 else th[2 * ax + c, w]

            def lowers(c, w):
                return nulls[2 * at + 1, 2 * ax + c, w]
        else:
            def links(c, w):
                return [sl[2 * at + c, ax, w + i] for i in range(4)]

            def uppers(c, w):
                return nulls[2 * at + c, 2, w] if ax == 0 else sh[2 * at + c, w]

            def lowers(c, w):
                return nulls[2 * at + c, 2 * ax + 1, w]
        slot = (at * 2 + ax) + (0 if kind == "t" else 4)
        for aw in range(8):
            for c in range(2):
                for i, image in enumerate(images(c, 4 * aw, links, uppers)):
                    k = (c * 2 + i) * 256
                    held[slot, aw, :, k:k + 128] = image[:16]
                    held[slot, aw, :, k + 128:k + 256] = image[16:]
        blocks = []
        for aw in range(8):
            left = jnp.concatenate([x for c in range(2) for x in conjugates(c, 4 * aw, lowers)], axis=1)
            blocks.append(dot_nt(left, held[slot, aw]))
        place(0 if kind == "t" else 1, at * 2 + ax, merge(blocks))

    def row_copy(half, to, slot):
        return pltpu.make_async_remote_copy(
            send.at[half, to], recv.at[half, me], row_send.at[half, to], row_recv.at[half, slot],
            device_id={"xyz": to}, device_id_type=MESH)

    def deliver(half):
        send[half] = dot_nn(pack[...], row_parts[half].astype(BF)).astype(BF).reshape(n_xyz, 16, 128)

        for peer in peers:
            row_copy(half, peer, me).start()

        pltpu.make_async_copy(send.at[half, me], recv.at[half, me], own_sem.at[half]).start()

    def collect(half):
        pltpu.make_async_copy(send.at[half, me], recv.at[half, me], own_sem.at[half]).wait()

        for peer in peers:
            row_copy(half, peer, peer).wait()

        placed = dot_nn(unpack[...], recv[half].reshape(512, 128))
        for q in range(4):
            out_ref[:, half * 512 + q * 128:half * 512 + (q + 1) * 128] = placed[q * 64:(q + 1) * 64].astype(BF)

    nulls_copy.wait()
    link_copies["s", 1, 1].wait()
    conjugate_through()
    pl.semaphore_wait(barrier, n_xyz + 1)
    halo = {}
    for name, src, dst, to in (
        ("w", through.at[0], through.at[1], {"xyz": up}),
        ("s", nulls_hbm.at[pl.ds(0, 2), 0], sh, {"xyz": down}),
        ("t0", nulls_hbm.at[0, pl.ds(0, 2)], th.at[pl.ds(0, 2)], {"ta": ta_down}),
        ("t1", nulls_hbm.at[0, pl.ds(2, 2)], th.at[pl.ds(2, 2)], {"ta": ta_down}),
        ("r", back.at[0], back.at[1], {"xyz": down}),
    ):
        i = len(halo)
        halo[name] = pltpu.make_async_remote_copy(
            src, dst, halo_send.at[i], halo_recv.at[i], device_id=to, device_id_type=MESH)
    for name in ("w", "s", "t0", "t1"):
        halo[name].start()

    for key in groups[1:]:
        link_copies[key].wait()
    group("t", 0, 0)
    group("t", 0, 1)
    group("s", 0, 0)
    group("s", 1, 0)
    halo["w"].wait()
    back[0] = merge([blocks_through(aw) for aw in range(8)]).astype(BF)
    halo["r"].start()
    halo["t0"].wait()
    group("t", 1, 0)
    halo["t1"].wait()
    group("t", 1, 1)
    deliver(0)
    halo["s"].wait()
    group("s", 0, 1)
    halo["r"].wait()
    place(1, 3, back[1].astype(F32))
    deliver(1)
    collect(0)
    collect(1)


def on_device(nulls, time_links, space_links, owner_lists):
    result = pl.pallas_call(
        kernel,
        out_shape=jax.ShapeDtypeStruct((64, 1024), BF),
        in_specs=[pl.BlockSpec(memory_space=pl.ANY)] * 3 + [pl.BlockSpec(memory_space=pltpu.VMEM)],
        out_specs=pl.BlockSpec(memory_space=pltpu.VMEM),
        scratch_shapes=[
            pltpu.VMEM((4, 4, 32, 16, 128), BF),
            pltpu.VMEM((2, 4, 32, 64, 128), BF),
            pltpu.VMEM((4, 2, 32, 64, 128), BF),
            pltpu.VMEM((4, 32, 16, 128), BF),
            pltpu.VMEM((2, 32, 16, 128), BF),
            pltpu.VMEM((8, 8, 16, 1024), BF),
            pltpu.VMEM((2, 128, 128), F32),
            pltpu.VMEM((2, 2, 32, 16, 128), BF),
            pltpu.VMEM((2, 32, 128), BF),
            pltpu.VMEM((32, 256), BF),
            pltpu.VMEM((512, 128), BF),
            pltpu.VMEM((256, 512), BF),
            pltpu.VMEM((2, 32, 16, 128), BF),
            pltpu.VMEM((2, 32, 16, 128), BF),
            pltpu.SemaphoreType.DMA,
            pltpu.SemaphoreType.DMA((8,)),
            pltpu.SemaphoreType.DMA((5,)),
            pltpu.SemaphoreType.DMA((5,)),
            pltpu.SemaphoreType.DMA((2, 32)),
            pltpu.SemaphoreType.DMA((2, 32)),
            pltpu.SemaphoreType.DMA((2,)),
        ],
        compiler_params=pltpu.CompilerParams(collective_id=0, has_side_effects=True),
    )(nulls, time_links, space_links, owner_lists)
    return result.astype(F32)[None]


def solution(mesh):
    return jax.shard_map(
        on_device,
        mesh=mesh,
        in_specs=(
            P("ta", "xyz", None, None, None),
            P("ta", "xyz", None, None, None),
            P("ta", "xyz", None, None, None),
            P(),
        ),
        out_specs=P("ta", "xyz", None),
        check_vma=False,
    )
```

```python
import functools

import jax
import jax.numpy as jnp
from jax import lax
from jax.experimental import pallas as pl
from jax.experimental.pallas import tpu as pltpu
from jax.sharding import PartitionSpec as P

MESH = pl.DeviceIdType.MESH
NY, NZ = 4, 8
ABOVE = 6
BF, F32, I32 = jnp.bfloat16, jnp.float32, jnp.int32


def dot_nt(a, b):
    return lax.dot_general(a, b, (((1,), (1,)), ((), ())), preferred_element_type=F32)


def dot_nn(a, b):
    return lax.dot_general(a, b, (((1,), (0,)), ((), ())), preferred_element_type=F32)


def iota(shape, dim):
    return lax.broadcasted_iota(I32, shape, dim)


def one_hot(cond):
    return jnp.where(cond, 1.0, 0.0).astype(BF)


def swap_halves(x):
    return jnp.concatenate([x[:, 64:], x[:, :64]], axis=1)


def kernel(
    nulls_hbm, tl_hbm, sl_hbm, owner_ref, out_ref,
    nulls, tl, sl, th, sh, held, row_parts, through, back, group_rows, pack, unpack, send, recv,
    link_sem, halo_send, halo_recv, row_send, row_recv, own_sem, met_sem,
):
    ta = lax.axis_index("ta")
    me = lax.axis_index("xyz")
    n_ta, n_xyz = 8, NY * NZ
    ta_down, ta_up = lax.rem(ta + n_ta - 1, n_ta), lax.rem(ta + 1, n_ta)
    down, up = lax.rem(me + n_xyz - 1, n_xyz), lax.rem(me + 1, n_xyz)
    my_y, my_z = lax.div(me, NZ), lax.rem(me, NZ)
    rows_y = [lax.rem(my_y + dy, NY) * NZ for dy in range(NY)]
    rows_z = [lax.rem(my_z + dz, NZ) for dz in range(NZ)]
    peers = [rows_y[dy] + rows_z[dz] for dz in (4, 3, 5, 2, 6, 1, 7, 0) for dy in (2, 1, 3, 0)][:-1]

    barrier = pltpu.get_barrier_semaphore()
    pl.semaphore_signal(barrier, inc=1, device_id={"ta": ta_down}, device_id_type=MESH)
    pl.semaphore_signal(barrier, inc=1, device_id={"ta": ta_up}, device_id_type=MESH)

    column = [rows_y[dy] + my_z for dy in (2, 1, 3)]
    ring = [rows_y[0] + rows_z[dz] for dz in (4, 3, 5, 2, 6, 1, 7)]
    for peer in [up, down] + ring + column:
        pl.semaphore_signal(barrier, inc=1, device_id={"xyz": peer}, device_id_type=MESH)

    def greet():
        for peer in column:
            pl.semaphore_signal(met_sem, inc=1, device_id={"xyz": peer}, device_id_type=MESH)

    copies = []

    def fetch(src, dst):
        copies.append(pltpu.make_async_copy(src, dst, link_sem.at[len(copies)]))
        copies[-1].start()

    cut = 4 * ABOVE
    fetch(nulls_hbm.at[pl.ds(2, 2), 3], nulls.at[pl.ds(2, 2), 3])
    fetch(sl_hbm.at[pl.ds(2, 2), 1, pl.ds(0, cut)], sl.at[pl.ds(2, 2), 1, pl.ds(0, cut)])

    def tables():
        row, col = iota((32, 256), 0), iota((32, 256), 1)
        group_rows[...] = one_hot(((row % 8) == (col // 32)) & ((row // 8) == ((col // 8) % 4)))
        lists = owner_ref[...]
        wide = jnp.broadcast_to(lists[:, None, :], (32, 16, 64)).reshape(512, 64)
        base = me * 32
        first = jnp.sum(jnp.where((wide >= 0) & (wide < base), 1, 0), axis=1, keepdims=True)
        r512 = iota((512, 1), 0)
        agg = jnp.sum(jnp.where(iota((512, 64), 1) == first + r512 % 4, wide, 0), axis=1, keepdims=True) - base
        target = jnp.where((agg >= 0) & (agg < 32), ((r512 // 4) % 4) * 32 + agg, -1)
        pack[...] = one_hot(iota((512, 128), 1) == target)
        mine = jnp.broadcast_to(owner_ref[pl.ds(me, 1), :], (256, 64))
        r256 = iota((256, 1), 0)
        slot = r256 % 64
        listed = jnp.sum(jnp.where(iota((256, 64), 1) == slot, mine, 0), axis=1, keepdims=True)
        place = jnp.where(listed >= 0, (listed // 32) * 16 + (r256 // 64) * 4 + slot % 4, -1)
        unpack[...] = one_hot(iota((256, 512), 1) == place)

    low16 = iota((16, 128), 1) < 64
    low32 = iota((32, 128), 1) < 64
    turn = jnp.where(low16, 1.0, -1.0).astype(BF)
    spread = one_hot(iota((16, 128), 0) == iota((16, 128), 1) % 16)
    keep = (iota((256, 128), 1) // 16) == (iota((256, 128), 0) % 8)
    none = jnp.zeros((32, 128), BF)

    def images(c, w, links, uppers):
        mats = links(c, w)
        weights = jnp.concatenate(
            [jnp.concatenate([mats[0], mats[2]], axis=0), jnp.concatenate([mats[1], mats[3]], axis=0)], axis=1)
        rows = []
        for i in range(4):
            v = uppers(c, w + i)
            paired = jnp.concatenate([v * turn, swap_halves(v)], axis=0)
            rows.append(jnp.concatenate([none, paired] if i % 2 else [paired, none], axis=1))
        product = dot_nt(jnp.concatenate(rows, axis=0), weights)
        for i in range(2):
            yield jnp.where(low32, product[32 * i:32 * i + 32], product[64 + 32 * i:96 + 32 * i]).astype(BF)

    def conjugates(c, w, lowers):
        for i in range(2):
            a, b = lowers(c, w + i), lowers(c, w + i + 2)
            re = jnp.where(low16, a, swap_halves(b))
            im = jnp.where(low16, swap_halves(a), b)
            yield jnp.concatenate([re, -im], axis=0)
            yield jnp.concatenate([im, re], axis=0)

    def merge(made):
        tiled = dot_nn(jnp.concatenate(made, axis=0).astype(BF), spread)
        return dot_nn(group_rows[...], jnp.where(keep, tiled, 0.0).astype(BF))

    def place(half, part, rows):
        for q in range(4):
            row_parts[half, pl.ds(q * 32 + part * 8, 8), :] = rows[8 * q:8 * q + 8]

    def conjugate_through():
        zero = jnp.zeros((16, 128), BF)
        for c in range(2):
            for w in range(0, cut, 4):
                rows = []
                for i in range(4):
                    v = nulls[2 + c, 3, w + i]
                    t = swap_halves(v)
                    if i % 2 == 0:
                        part = jnp.concatenate([jnp.where(low16, v, zero), jnp.where(low16, t, zero)], axis=0)
                    else:
                        part = jnp.concatenate([jnp.where(low16, zero, t), jnp.where(low16, zero, v)], axis=0)
                    rows.append(jnp.concatenate([part, none] if i < 2 else [none, part], axis=1))
                weights = jnp.concatenate([sl[2 + c, 1, w + i] for i in range(4)], axis=0)
                product = dot_nn(jnp.concatenate(rows, axis=0), weights)
                for i in range(4):
                    top, low = product[32 * i:32 * i + 16], product[32 * i + 16:32 * i + 32]
                    through[0, c, w + i] = (top + jnp.where(low16, swap_halves(low), -swap_halves(low))).astype(BF)

    def blocks_through(aw):
        left, right = [], []
        for c in range(2):
            for w in range(4 * aw, 4 * aw + 4):
                v = through[1, c, w]
                left.append(jnp.concatenate([v * turn, swap_halves(v)], axis=0))
                right.append(nulls[2 + c, 0, w])
        return dot_nt(jnp.concatenate(left, axis=1), jnp.concatenate(right, axis=1))

    def group(kind, at, ax):
        place(0 if kind == "t" else 1, at * 2 + ax, merge(blocks(kind, at, ax, range(8))))

    def blocks(kind, at, ax, which):
        if kind == "t":
            def links(c, w):
                return [tl[at, 2 * ax + c, w + i] for i in range(4)]

            def uppers(c, w):
                return nulls[2, 2 * ax + c, w] if at == 0 else th[2 * ax + c, w]

            def lowers(c, w):
                return nulls[2 * at + 1, 2 * ax + c, w]
        else:
            def links(c, w):
                return [sl[2 * at + c, ax, w + i] for i in range(4)]

            def uppers(c, w):
                return nulls[2 * at + c, 2, w] if ax == 0 else sh[2 * at + c, w]

            def lowers(c, w):
                return nulls[2 * at + c, 2 * ax + 1, w]
        slot = (at * 2 + ax) + (0 if kind == "t" else 4)
        for aw in which:
            for c in range(2):
                for i, image in enumerate(images(c, 4 * aw, links, uppers)):
                    k = (c * 2 + i) * 256
                    held[slot, aw, :, k:k + 128] = image[:16]
                    held[slot, aw, :, k + 128:k + 256] = image[16:]
        made = []
        for aw in which:
            left = jnp.concatenate([x for c in range(2) for x in conjugates(c, 4 * aw, lowers)], axis=1)
            made.append(dot_nt(left, held[slot, aw]))
        return made

    def row_copy(half, to, slot):
        return pltpu.make_async_remote_copy(
            send.at[half, to], recv.at[half, me], row_send.at[half, to], row_recv.at[half, slot],
            device_id={"xyz": to}, device_id_type=MESH)

    def deliver(half):
        send[half] = dot_nn(pack[...], row_parts[half].astype(BF)).astype(BF).reshape(n_xyz, 16, 128)

        for peer in peers:
            row_copy(half, peer, me).start()

        pltpu.make_async_copy(send.at[half, me], recv.at[half, me], own_sem.at[half]).start()

    def collect(half):
        pltpu.make_async_copy(send.at[half, me], recv.at[half, me], own_sem.at[half]).wait()

        for peer in peers:
            row_copy(half, peer, peer).wait()

        placed = dot_nn(unpack[...], recv[half].reshape(512, 128))
        for q in range(4):
            out_ref[:, half * 512 + q * 128:half * 512 + (q + 1) * 128] = placed[q * 64:(q + 1) * 64].astype(BF)

    pl.semaphore_wait(barrier, 14)
    halo = {}
    for name, src, dst, to in (
        ("w", through.at[0], through.at[1], {"xyz": up}),
        ("s1", nulls_hbm.at[pl.ds(2, 2), 0, pl.ds(cut, 32 - cut)], sh.at[pl.ds(2, 2), pl.ds(cut, 32 - cut)], {"xyz": down}),
        ("s0", nulls_hbm.at[pl.ds(0, 2), 0], sh.at[pl.ds(0, 2)], {"xyz": down}),
        ("t0", nulls_hbm.at[0, pl.ds(0, 2)], th.at[pl.ds(0, 2)], {"ta": ta_down}),
        ("t1", nulls_hbm.at[0, pl.ds(2, 2)], th.at[pl.ds(2, 2)], {"ta": ta_down}),
        ("r", back.at[0], back.at[1], {"xyz": down}),
    ):
        i = len(halo)
        halo[name] = pltpu.make_async_remote_copy(
            src, dst, halo_send.at[i], halo_recv.at[i], device_id=to, device_id_type=MESH)
    for name in ("s1", "s0", "t0", "t1"):
        halo[name].start()
    greet()
    copies[0].wait()
    copies[1].wait()
    conjugate_through()
    halo["w"].start()
    fetch(nulls_hbm.at[pl.ds(2, 2), pl.ds(0, 3)], nulls.at[pl.ds(2, 2), pl.ds(0, 3)])
    fetch(nulls_hbm.at[pl.ds(0, 2)], nulls.at[pl.ds(0, 2)])
    for at in range(2):
        fetch(tl_hbm.at[at], tl.at[at])
    fetch(sl_hbm.at[pl.ds(0, 2)], sl.at[pl.ds(0, 2)])
    fetch(sl_hbm.at[pl.ds(2, 2), 0], sl.at[pl.ds(2, 2), 0])
    fetch(sl_hbm.at[pl.ds(2, 2), 1, pl.ds(cut, 32 - cut)], sl.at[pl.ds(2, 2), 1, pl.ds(cut, 32 - cut)])
    tables()
    for copy in copies[2:]:
        copy.wait()
    group("t", 0, 0)
    group("t", 0, 1)
    group("s", 0, 0)
    group("s", 1, 0)
    nil = [jnp.zeros((32, 16), F32)]
    halo["w"].wait()
    back[0] = merge([blocks_through(aw) for aw in range(ABOVE)] + nil * (8 - ABOVE)).astype(BF)
    halo["r"].start()
    halo["t0"].wait()
    group("t", 1, 0)
    halo["t1"].wait()
    group("t", 1, 1)
    pl.semaphore_wait(met_sem, 3)
    deliver(0)
    halo["s1"].wait()
    own = merge(nil * ABOVE + blocks("s", 1, 1, range(ABOVE, 8)))
    halo["s0"].wait()
    group("s", 0, 1)
    halo["r"].wait()
    place(1, 3, own + back[1].astype(F32))
    deliver(1)
    collect(0)
    collect(1)


def on_device(nulls, time_links, space_links, owner_lists):
    result = pl.pallas_call(
        kernel,
        out_shape=pltpu.VMEM((64, 1024), BF),
        in_specs=[pl.BlockSpec(memory_space=pl.ANY)] * 3 + [pl.BlockSpec(memory_space=pltpu.VMEM)],
        out_specs=pl.BlockSpec(memory_space=pltpu.VMEM),
        scratch_shapes=[
            pltpu.VMEM((4, 4, 32, 16, 128), BF),
            pltpu.VMEM((2, 4, 32, 64, 128), BF),
            pltpu.VMEM((4, 2, 32, 64, 128), BF),
            pltpu.VMEM((4, 32, 16, 128), BF),
            pltpu.VMEM((4, 32, 16, 128), BF),
            pltpu.VMEM((8, 8, 16, 1024), BF),
            pltpu.VMEM((2, 128, 128), F32),
            pltpu.VMEM((2, 2, 4 * ABOVE, 16, 128), BF),
            pltpu.VMEM((2, 32, 128), BF),
            pltpu.VMEM((32, 256), BF),
            pltpu.VMEM((512, 128), BF),
            pltpu.VMEM((256, 512), BF),
            pltpu.VMEM((2, 32, 16, 128), BF),
            pltpu.VMEM((2, 32, 16, 128), BF),
            pltpu.SemaphoreType.DMA((9,)),
            pltpu.SemaphoreType.DMA((6,)),
            pltpu.SemaphoreType.DMA((6,)),
            pltpu.SemaphoreType.DMA((2, 32)),
            pltpu.SemaphoreType.DMA((2, 32)),
            pltpu.SemaphoreType.DMA((2,)),
            pltpu.SemaphoreType.REGULAR,
        ],
        compiler_params=pltpu.CompilerParams(collective_id=0, has_side_effects=True),
    )(nulls, time_links, space_links, owner_lists)
    return result.astype(F32)[None]


def solution(mesh):
    return jax.shard_map(
        on_device,
        mesh=mesh,
        in_specs=(
            P("ta", "xyz", None, None, None),
            P("ta", "xyz", None, None, None),
            P("ta", "xyz", None, None, None),
            P(),
        ),
        out_specs=P("ta", "xyz", None),
        check_vma=False,
    )
```

```python
import functools

import jax
import jax.numpy as jnp
from jax import lax
from jax.experimental import pallas as pl
from jax.experimental.pallas import tpu as pltpu
from jax.sharding import PartitionSpec as P

MESH = pl.DeviceIdType.MESH
NY, NZ = 4, 8
ABOVE = 6
BF, F32, I32 = jnp.bfloat16, jnp.float32, jnp.int32


def dot_nt(a, b):
    return lax.dot_general(a, b, (((1,), (1,)), ((), ())), preferred_element_type=F32)


def dot_nn(a, b):
    return lax.dot_general(a, b, (((1,), (0,)), ((), ())), preferred_element_type=F32)


def iota(shape, dim):
    return lax.broadcasted_iota(I32, shape, dim)


def one_hot(cond):
    return jnp.where(cond, 1.0, 0.0).astype(BF)


def swap_halves(x):
    return jnp.concatenate([x[:, 64:], x[:, :64]], axis=1)


def kernel(
    nulls_hbm, tl_hbm, sl_hbm, owner_ref, out_ref,
    nulls, tl, sl, th, sh, held, row_parts, through, back, group_rows, pack, unpack, send, recv,
    link_sem, halo_send, halo_recv, row_send, row_recv, met_sem,
):
    ta = lax.axis_index("ta")
    me = lax.axis_index("xyz")
    n_ta, n_xyz = 8, NY * NZ
    ta_down, ta_up = lax.rem(ta + n_ta - 1, n_ta), lax.rem(ta + 1, n_ta)
    down, up = lax.rem(me + n_xyz - 1, n_xyz), lax.rem(me + 1, n_xyz)
    my_y, my_z = lax.div(me, NZ), lax.rem(me, NZ)
    rows_y = [lax.rem(my_y + dy, NY) * NZ for dy in range(NY)]
    rows_z = [lax.rem(my_z + dz, NZ) for dz in range(NZ)]
    peers = [rows_y[dy] + rows_z[dz] for dz in (4, 3, 5, 2, 6, 1, 7, 0) for dy in (2, 1, 3, 0)][:-1]

    barrier = pltpu.get_barrier_semaphore()
    pl.semaphore_signal(barrier, inc=1, device_id={"ta": ta_down}, device_id_type=MESH)
    pl.semaphore_signal(barrier, inc=1, device_id={"ta": ta_up}, device_id_type=MESH)

    column = [rows_y[dy] + my_z for dy in (2, 1, 3)]
    ring = [rows_y[0] + rows_z[dz] for dz in (4, 3, 5, 2, 6, 1, 7)]
    for peer in [up, down] + ring + column:
        pl.semaphore_signal(barrier, inc=1, device_id={"xyz": peer}, device_id_type=MESH)

    def greet():
        for peer in column:
            pl.semaphore_signal(met_sem, inc=1, device_id={"xyz": peer}, device_id_type=MESH)

    copies = []

    def fetch(src, dst):
        copies.append(pltpu.make_async_copy(src, dst, link_sem.at[len(copies)]))
        copies[-1].start()

    cut = 4 * ABOVE
    fetch(nulls_hbm.at[pl.ds(2, 2), 3], nulls.at[pl.ds(2, 2), 3])
    fetch(sl_hbm.at[pl.ds(2, 2), 1, pl.ds(0, cut)], sl.at[pl.ds(2, 2), 1, pl.ds(0, cut)])

    def packing():
        row, col = iota((32, 256), 0), iota((32, 256), 1)
        group_rows[...] = one_hot(((row % 8) == (col // 32)) & ((row // 8) == ((col // 8) % 4)))
        lists = owner_ref[...]
        base = me * 32
        place = iota((32, 64), 1)
        first = jnp.sum(jnp.where((lists >= 0) & (lists < base), 1, 0), axis=1, keepdims=True)
        lane = iota((32, 128), 1)
        picks = []
        for r in range(4):
            agg = jnp.sum(jnp.where(place == first + r, lists, 0), axis=1, keepdims=True) - base
            picks.append(one_hot((lane % 32 == agg) & (agg >= 0) & (agg < 32)))
        row, col = iota((512, 128), 0), iota((512, 128), 1)
        spreader = one_hot((row // 16 == col % 32) & (row % 4 == col // 32))
        wide = dot_nn(spreader, jnp.concatenate(picks, axis=0))
        pack[...] = jnp.where((row // 4) % 4 == col // 32, wide, 0.0).astype(BF)

    def unpacking():
        mine = jnp.broadcast_to(owner_ref[pl.ds(me, 1), :], (64, 64))
        r64 = iota((64, 1), 0)
        listed = jnp.sum(jnp.where(iota((64, 64), 1) == r64, mine, 0), axis=1, keepdims=True)
        place = jnp.where(listed >= 0, (listed // 32) * 16 + r64 % 4, -4 * 16)
        col = iota((64, 512), 1)
        for q in range(4):
            unpack[pl.ds(64 * q, 64), :] = one_hot(col == place + 4 * q)

    low16 = iota((16, 128), 1) < 64
    low32 = iota((32, 128), 1) < 64
    turn = jnp.where(low16, 1.0, -1.0).astype(BF)
    spread = one_hot(iota((16, 128), 0) == iota((16, 128), 1) % 16)
    keep = (iota((256, 128), 1) // 16) == (iota((256, 128), 0) % 8)
    none = jnp.zeros((32, 128), BF)

    def images(c, w, links, uppers):
        mats = links(c, w)
        weights = jnp.concatenate(
            [jnp.concatenate([mats[0], mats[2]], axis=0), jnp.concatenate([mats[1], mats[3]], axis=0)], axis=1)
        rows = []
        for i in range(4):
            v = uppers(c, w + i)
            paired = jnp.concatenate([v * turn, swap_halves(v)], axis=0)
            rows.append(jnp.concatenate([none, paired] if i % 2 else [paired, none], axis=1))
        product = dot_nt(jnp.concatenate(rows, axis=0), weights)
        for i in range(2):
            yield jnp.where(low32, product[32 * i:32 * i + 32], product[64 + 32 * i:96 + 32 * i]).astype(BF)

    def conjugates(c, w, lowers):
        for i in range(2):
            a, b = lowers(c, w + i), lowers(c, w + i + 2)
            re = jnp.where(low16, a, swap_halves(b))
            im = jnp.where(low16, swap_halves(a), b)
            yield jnp.concatenate([re, -im], axis=0)
            yield jnp.concatenate([im, re], axis=0)

    def merge(made):
        tiled = dot_nn(jnp.concatenate(made, axis=0).astype(BF), spread)
        return dot_nn(group_rows[...], jnp.where(keep, tiled, 0.0).astype(BF))

    def place(half, part, rows):
        for q in range(4):
            row_parts[half, pl.ds(q * 32 + part * 8, 8), :] = rows[8 * q:8 * q + 8]

    def conjugate_through():
        zero = jnp.zeros((16, 128), BF)
        for c in range(2):
            for w in range(0, cut, 4):
                rows = []
                for i in range(4):
                    v = nulls[2 + c, 3, w + i]
                    t = swap_halves(v)
                    if i % 2 == 0:
                        part = jnp.concatenate([jnp.where(low16, v, zero), jnp.where(low16, t, zero)], axis=0)
                    else:
                        part = jnp.concatenate([jnp.where(low16, zero, t), jnp.where(low16, zero, v)], axis=0)
                    rows.append(jnp.concatenate([part, none] if i < 2 else [none, part], axis=1))
                weights = jnp.concatenate([sl[2 + c, 1, w + i] for i in range(4)], axis=0)
                product = dot_nn(jnp.concatenate(rows, axis=0), weights)
                for i in range(4):
                    top, low = product[32 * i:32 * i + 16], product[32 * i + 16:32 * i + 32]
                    through[0, c, w + i] = (top + jnp.where(low16, swap_halves(low), -swap_halves(low))).astype(BF)

    def blocks_through(aw):
        left, right = [], []
        for c in range(2):
            for w in range(4 * aw, 4 * aw + 4):
                v = through[1, c, w]
                left.append(jnp.concatenate([v * turn, swap_halves(v)], axis=0))
                right.append(nulls[2 + c, 0, w])
        return dot_nt(jnp.concatenate(left, axis=1), jnp.concatenate(right, axis=1))

    def group(kind, at, ax):
        place(0 if kind == "t" else 1, at * 2 + ax, merge(blocks(kind, at, ax, range(8))))

    def blocks(kind, at, ax, which):
        if kind == "t":
            def links(c, w):
                return [tl[at, 2 * ax + c, w + i] for i in range(4)]

            def uppers(c, w):
                return nulls[2, 2 * ax + c, w] if at == 0 else th[2 * ax + c, w]

            def lowers(c, w):
                return nulls[2 * at + 1, 2 * ax + c, w]
        else:
            def links(c, w):
                return [sl[2 * at + c, ax, w + i] for i in range(4)]

            def uppers(c, w):
                return nulls[2 * at + c, 2, w] if ax == 0 else sh[2 * at + c, w]

            def lowers(c, w):
                return nulls[2 * at + c, 2 * ax + 1, w]
        slot = (at * 2 + ax) + (0 if kind == "t" else 4)
        for aw in which:
            for c in range(2):
                for i, image in enumerate(images(c, 4 * aw, links, uppers)):
                    k = (c * 2 + i) * 256
                    held[slot, aw, :, k:k + 128] = image[:16]
                    held[slot, aw, :, k + 128:k + 256] = image[16:]
        made = []
        for aw in which:
            left = jnp.concatenate([x for c in range(2) for x in conjugates(c, 4 * aw, lowers)], axis=1)
            made.append(dot_nt(left, held[slot, aw]))
        return made

    def deliver(half):
        send[half] = dot_nn(pack[...], row_parts[half].astype(BF)).astype(BF).reshape(n_xyz, 16, 128)
        for peer in peers:
            pltpu.make_async_remote_copy(
                send.at[half, peer], recv.at[half, me], row_send.at[half], row_recv.at[half],
                device_id={"xyz": peer}, device_id_type=MESH).start()
        pltpu.make_async_copy(send.at[half, me], recv.at[half, me], row_recv.at[half]).start()

    def collect(half):
        pltpu.make_async_copy(recv.at[half], recv.at[half], row_recv.at[half]).wait()
        placed = dot_nn(unpack[...], recv[half].reshape(512, 128))
        for q in range(4):
            out_ref[:, half * 512 + q * 128:half * 512 + (q + 1) * 128] = placed[q * 64:(q + 1) * 64].astype(BF)

    fetch(nulls_hbm.at[pl.ds(0, 2)], nulls.at[pl.ds(0, 2)])
    fetch(nulls_hbm.at[pl.ds(2, 2), pl.ds(0, 3)], nulls.at[pl.ds(2, 2), pl.ds(0, 3)])
    fetch(tl_hbm.at[0], tl.at[0])
    fetch(sl_hbm.at[pl.ds(0, 2), 0], sl.at[pl.ds(0, 2), 0])
    fetch(sl_hbm.at[pl.ds(2, 2), 0], sl.at[pl.ds(2, 2), 0])
    fetch(tl_hbm.at[1], tl.at[1])
    fetch(sl_hbm.at[pl.ds(0, 2), 1], sl.at[pl.ds(0, 2), 1])
    fetch(sl_hbm.at[pl.ds(2, 2), 1, pl.ds(cut, 32 - cut)], sl.at[pl.ds(2, 2), 1, pl.ds(cut, 32 - cut)])
    pl.semaphore_wait(barrier, 14)
    halo = {}
    for name, src, dst, to in (
        ("w", through.at[0], through.at[1], {"xyz": up}),
        ("s1", nulls_hbm.at[pl.ds(2, 2), 0, pl.ds(cut, 32 - cut)], sh.at[pl.ds(2, 2), pl.ds(cut, 32 - cut)], {"xyz": down}),
        ("s0", nulls_hbm.at[pl.ds(0, 2), 0], sh.at[pl.ds(0, 2)], {"xyz": down}),
        ("t0", nulls_hbm.at[0, pl.ds(0, 2)], th.at[pl.ds(0, 2)], {"ta": ta_down}),
        ("t1", nulls_hbm.at[0, pl.ds(2, 2)], th.at[pl.ds(2, 2)], {"ta": ta_down}),
        ("r", back.at[0], back.at[1], {"xyz": down}),
    ):
        i = len(halo)
        halo[name] = pltpu.make_async_remote_copy(
            src, dst, halo_send.at[i], halo_recv.at[i], device_id=to, device_id_type=MESH)
    for name in ("s1", "s0", "t0", "t1"):
        halo[name].start()
    greet()
    copies[0].wait()
    copies[1].wait()
    conjugate_through()
    halo["w"].start()
    packing()
    for copy in copies[2:5]:
        copy.wait()
    group("t", 0, 0)
    group("t", 0, 1)
    copies[5].wait()
    copies[6].wait()
    group("s", 0, 0)
    group("s", 1, 0)
    nil = [jnp.zeros((32, 16), F32)]
    halo["w"].wait()
    back[0] = merge([blocks_through(aw) for aw in range(ABOVE)] + nil * (8 - ABOVE)).astype(BF)
    halo["r"].start()
    copies[7].wait()
    halo["t0"].wait()
    halo["t1"].wait()
    group("t", 1, 0)
    group("t", 1, 1)
    pl.semaphore_wait(met_sem, 3)
    deliver(0)
    copies[8].wait()
    copies[9].wait()
    halo["s1"].wait()
    own = merge(nil * ABOVE + blocks("s", 1, 1, range(ABOVE, 8)))
    halo["s0"].wait()
    group("s", 0, 1)
    halo["r"].wait()
    place(1, 3, own + back[1].astype(F32))
    deliver(1)
    unpacking()
    collect(0)
    collect(1)
    for half in range(2):
        most = send.at[half, pl.ds(0, n_xyz - 1)]
        pltpu.make_async_copy(most, most, row_send.at[half]).wait()


def on_device(nulls, time_links, space_links, owner_lists):
    result = pl.pallas_call(
        kernel,
        out_shape=pltpu.VMEM((64, 1024), BF),
        in_specs=[pl.BlockSpec(memory_space=pl.ANY)] * 3 + [pl.BlockSpec(memory_space=pltpu.VMEM)],
        out_specs=pl.BlockSpec(memory_space=pltpu.VMEM),
        scratch_shapes=[
            pltpu.VMEM((4, 4, 32, 16, 128), BF),
            pltpu.VMEM((2, 4, 32, 64, 128), BF),
            pltpu.VMEM((4, 2, 32, 64, 128), BF),
            pltpu.VMEM((4, 32, 16, 128), BF),
            pltpu.VMEM((4, 32, 16, 128), BF),
            pltpu.VMEM((8, 8, 16, 1024), BF),
            pltpu.VMEM((2, 128, 128), F32),
            pltpu.VMEM((2, 2, 4 * ABOVE, 16, 128), BF),
            pltpu.VMEM((2, 32, 128), BF),
            pltpu.VMEM((32, 256), BF),
            pltpu.VMEM((512, 128), BF),
            pltpu.VMEM((256, 512), BF),
            pltpu.VMEM((2, 32, 16, 128), BF),
            pltpu.VMEM((2, 32, 16, 128), BF),
            pltpu.SemaphoreType.DMA((10,)),
            pltpu.SemaphoreType.DMA((6,)),
            pltpu.SemaphoreType.DMA((6,)),
            pltpu.SemaphoreType.DMA((2,)),
            pltpu.SemaphoreType.DMA((2,)),
            pltpu.SemaphoreType.REGULAR,
        ],
        compiler_params=pltpu.CompilerParams(collective_id=0, has_side_effects=True),
    )(nulls, time_links, space_links, owner_lists)
    return result.astype(F32)[None]


def solution(mesh):
    return jax.shard_map(
        on_device,
        mesh=mesh,
        in_specs=(
            P("ta", "xyz", None, None, None),
            P("ta", "xyz", None, None, None),
            P("ta", "xyz", None, None, None),
            P(),
        ),
        out_specs=P("ta", "xyz", None),
        check_vma=False,
    )
```

```python
import functools

import jax
import jax.numpy as jnp
from jax import lax
from jax.experimental import pallas as pl
from jax.experimental.pallas import tpu as pltpu
from jax.sharding import PartitionSpec as P

MESH = pl.DeviceIdType.MESH
NY, NZ = 4, 8
ABOVE = 6
BF, F32, I32 = jnp.bfloat16, jnp.float32, jnp.int32


def dot_nt(a, b):
    return lax.dot_general(a, b, (((1,), (1,)), ((), ())), preferred_element_type=F32)


def dot_nn(a, b):
    return lax.dot_general(a, b, (((1,), (0,)), ((), ())), preferred_element_type=F32)


def iota(shape, dim):
    return lax.broadcasted_iota(I32, shape, dim)


def one_hot(cond):
    return jnp.where(cond, 1.0, 0.0).astype(BF)


def swap_halves(x):
    return jnp.concatenate([x[:, 64:], x[:, :64]], axis=1)


def kernel(
    nulls_hbm, tl_hbm, sl_hbm, owner_ref, out_ref,
    nulls, tl, sl, th, sh, held, row_parts, through, back, group_rows, pack, unpack, send, recv,
    link_sem, halo_send, halo_recv, row_send, row_recv, met_sem,
):
    ta = lax.axis_index("ta")
    me = lax.axis_index("xyz")
    n_ta, n_xyz = 8, NY * NZ
    ta_down, ta_up = lax.rem(ta + n_ta - 1, n_ta), lax.rem(ta + 1, n_ta)
    down, up = lax.rem(me + n_xyz - 1, n_xyz), lax.rem(me + 1, n_xyz)
    my_y, my_z = lax.div(me, NZ), lax.rem(me, NZ)
    rows_y = [lax.rem(my_y + dy, NY) * NZ for dy in range(NY)]
    rows_z = [lax.rem(my_z + dz, NZ) for dz in range(NZ)]
    peers = [rows_y[dy] + rows_z[dz] for dz in (4, 3, 5, 2, 6, 1, 7, 0) for dy in (2, 1, 3, 0)][:-1]

    barrier = pltpu.get_barrier_semaphore()
    pl.semaphore_signal(barrier, inc=1, device_id={"ta": ta_down}, device_id_type=MESH)
    pl.semaphore_signal(barrier, inc=1, device_id={"ta": ta_up}, device_id_type=MESH)

    column = [rows_y[dy] + my_z for dy in (2, 1, 3)]
    ring = [rows_y[0] + rows_z[dz] for dz in (2, 6, 1, 7)]
    for peer in [up, down] + ring + column:
        pl.semaphore_signal(barrier, inc=1, device_id={"xyz": peer}, device_id_type=MESH)

    def greet(level):
        for peer in column + (ring[:2] if level == 0 else []):
            pl.semaphore_signal(met_sem.at[level], inc=1, device_id={"xyz": peer}, device_id_type=MESH)

    loads = {}

    def fetch(name, src, dst):
        loads[name] = pltpu.make_async_copy(src, dst, link_sem.at[len(loads)])
        loads[name].start()

    cut = 4 * ABOVE
    early, late = pl.ds(0, cut), pl.ds(cut, 32 - cut)
    low, high = pl.ds(0, 2), pl.ds(2, 2)
    fetch("n0", nulls_hbm.at[high, 3], nulls.at[high, 3])
    fetch("s11", sl_hbm.at[high, 1, early], sl.at[high, 1, early])
    fetch("n1", nulls_hbm.at[3, 2], nulls.at[3, 2])
    fetch("t11", tl_hbm.at[1, high, early], tl.at[1, high, early])
    fetch("n2", nulls_hbm.at[low], nulls.at[low])
    fetch("n3", nulls_hbm.at[high, low], nulls.at[high, low])
    fetch("n4", nulls_hbm.at[2, 2], nulls.at[2, 2])
    fetch("t0", tl_hbm.at[0], tl.at[0])
    fetch("s00", sl_hbm.at[low, 0], sl.at[low, 0])
    fetch("s10", sl_hbm.at[high, 0], sl.at[high, 0])
    fetch("t10", tl_hbm.at[1, low], tl.at[1, low])
    fetch("s01", sl_hbm.at[low, 1], sl.at[low, 1])
    fetch("t11b", tl_hbm.at[1, high, late], tl.at[1, high, late])
    fetch("s11b", sl_hbm.at[high, 1, late], sl.at[high, 1, late])

    def packing():
        row, col = iota((32, 256), 0), iota((32, 256), 1)
        group_rows[...] = one_hot(((row % 8) == (col // 32)) & ((row // 8) == ((col // 8) % 4)))
        lists = owner_ref[...]
        base = me * 32
        place = iota((32, 64), 1)
        first = jnp.sum(jnp.where((lists >= 0) & (lists < base), 1, 0), axis=1, keepdims=True)
        lane = iota((32, 128), 1)
        picks = []
        for r in range(4):
            agg = jnp.sum(jnp.where(place == first + r, lists, 0), axis=1, keepdims=True) - base
            picks.append(one_hot((lane % 32 == agg) & (agg >= 0) & (agg < 32)))
        row, col = iota((512, 128), 0), iota((512, 128), 1)
        spreader = one_hot((row // 16 == col % 32) & (row % 4 == col // 32))
        wide = dot_nn(spreader, jnp.concatenate(picks, axis=0))
        pack[...] = jnp.where((row // 4) % 4 == col // 32, wide, 0.0).astype(BF)

    def unpacking():
        mine = jnp.broadcast_to(owner_ref[pl.ds(me, 1), :], (64, 64))
        r64 = iota((64, 1), 0)
        listed = jnp.sum(jnp.where(iota((64, 64), 1) == r64, mine, 0), axis=1, keepdims=True)
        place = jnp.where(listed >= 0, (listed // 32) * 16 + r64 % 4, -4 * 16)
        col = iota((64, 512), 1)
        for q in range(4):
            unpack[pl.ds(64 * q, 64), :] = one_hot(col == place + 4 * q)

    low16 = iota((16, 128), 1) < 64
    low32 = iota((32, 128), 1) < 64
    turn = jnp.where(low16, 1.0, -1.0).astype(BF)
    spread = one_hot(iota((16, 128), 0) == iota((16, 128), 1) % 16)
    keep = (iota((256, 128), 1) // 16) == (iota((256, 128), 0) % 8)
    none = jnp.zeros((32, 128), BF)

    def images(c, w, links, uppers):
        mats = links(c, w)
        weights = jnp.concatenate(
            [jnp.concatenate([mats[0], mats[2]], axis=0), jnp.concatenate([mats[1], mats[3]], axis=0)], axis=1)
        rows = []
        for i in range(4):
            v = uppers(c, w + i)
            paired = jnp.concatenate([v * turn, swap_halves(v)], axis=0)
            rows.append(jnp.concatenate([none, paired] if i % 2 else [paired, none], axis=1))
        product = dot_nt(jnp.concatenate(rows, axis=0), weights)
        for i in range(2):
            yield jnp.where(low32, product[32 * i:32 * i + 32], product[64 + 32 * i:96 + 32 * i]).astype(BF)

    def conjugates(c, w, lowers):
        for i in range(2):
            a, b = lowers(c, w + i), lowers(c, w + i + 2)
            re = jnp.where(low16, a, swap_halves(b))
            im = jnp.where(low16, swap_halves(a), b)
            yield jnp.concatenate([re, -im], axis=0)
            yield jnp.concatenate([im, re], axis=0)

    def merge(made):
        tiled = dot_nn(jnp.concatenate(made, axis=0).astype(BF), spread)
        return dot_nn(group_rows[...], jnp.where(keep, tiled, 0.0).astype(BF))

    def place(half, part, rows):
        for q in range(4):
            row_parts[half, pl.ds(q * 32 + part * 8, 8), :] = rows[8 * q:8 * q + 8]

    def conjugate_through(half):
        zero = jnp.zeros((16, 128), BF)
        for c in range(2):
            for w in range(0, cut, 4):
                rows = []
                for i in range(4):
                    v = nulls[2 + c, 3, w + i] if half else nulls[3, 2 + c, w + i]
                    t = swap_halves(v)
                    if i % 2 == 0:
                        part = jnp.concatenate([jnp.where(low16, v, zero), jnp.where(low16, t, zero)], axis=0)
                    else:
                        part = jnp.concatenate([jnp.where(low16, zero, t), jnp.where(low16, zero, v)], axis=0)
                    rows.append(jnp.concatenate([part, none] if i < 2 else [none, part], axis=1))
                mats = [sl[2 + c, 1, w + i] if half else tl[1, 2 + c, w + i] for i in range(4)]
                weights = jnp.concatenate(mats, axis=0)
                product = dot_nn(jnp.concatenate(rows, axis=0), weights)
                for i in range(4):
                    top, low = product[32 * i:32 * i + 16], product[32 * i + 16:32 * i + 32]
                    through[half, 0, c, w + i] = (top + jnp.where(low16, swap_halves(low), -swap_halves(low))).astype(BF)

    def blocks_through(half, aw):
        left, right = [], []
        for c in range(2):
            for w in range(4 * aw, 4 * aw + 4):
                v = through[half, 1, c, w]
                left.append(jnp.concatenate([v * turn, swap_halves(v)], axis=0))
                right.append(nulls[2 + c, 0, w] if half else nulls[0, 2 + c, w])
        return dot_nt(jnp.concatenate(left, axis=1), jnp.concatenate(right, axis=1))

    def group(kind, at, ax):
        place(0 if kind == "t" else 1, at * 2 + ax, merge(blocks(kind, at, ax, range(8))))

    def blocks(kind, at, ax, which):
        if kind == "t":
            def links(c, w):
                return [tl[at, 2 * ax + c, w + i] for i in range(4)]

            def uppers(c, w):
                return nulls[2, 2 * ax + c, w] if at == 0 else th[2 * ax + c, w]

            def lowers(c, w):
                return nulls[2 * at + 1, 2 * ax + c, w]
        else:
            def links(c, w):
                return [sl[2 * at + c, ax, w + i] for i in range(4)]

            def uppers(c, w):
                return nulls[2 * at + c, 2, w] if ax == 0 else sh[2 * at + c, w]

            def lowers(c, w):
                return nulls[2 * at + c, 2 * ax + 1, w]
        slot = (at * 2 + ax) + (0 if kind == "t" else 4)
        for aw in which:
            for c in range(2):
                for i, image in enumerate(images(c, 4 * aw, links, uppers)):
                    k = (c * 2 + i) * 256
                    held[slot, aw, :, k:k + 128] = image[:16]
                    held[slot, aw, :, k + 128:k + 256] = image[16:]
        made = []
        for aw in which:
            left = jnp.concatenate([x for c in range(2) for x in conjugates(c, 4 * aw, lowers)], axis=1)
            made.append(dot_nt(left, held[slot, aw]))
        return made

    def deliver(half):
        send[half] = dot_nn(pack[...], row_parts[half].astype(BF)).astype(BF).reshape(n_xyz, 16, 128)
        for peer in peers:
            pltpu.make_async_remote_copy(
                send.at[half, peer], recv.at[half, me], row_send.at[half], row_recv.at[half],
                device_id={"xyz": peer}, device_id_type=MESH).start()
        pltpu.make_async_copy(send.at[half, me], recv.at[half, me], row_recv.at[half]).start()

    def collect(half):
        pltpu.make_async_copy(recv.at[half], recv.at[half], row_recv.at[half]).wait()
        placed = dot_nn(unpack[...], recv[half].reshape(512, 128))
        for q in range(4):
            out_ref[:, half * 512 + q * 128:half * 512 + (q + 1) * 128] = placed[q * 64:(q + 1) * 64].astype(BF)

    pl.semaphore_wait(barrier, 11)
    halo = {}
    for name, src, dst, to in (
        ("t0", nulls_hbm.at[0, low], th.at[low], {"ta": ta_down}),
        ("t1", nulls_hbm.at[0, high, late], th.at[high, late], {"ta": ta_down}),
        ("s1", nulls_hbm.at[high, 0, late], sh.at[high, late], {"xyz": down}),
        ("s0", nulls_hbm.at[low, 0], sh.at[low], {"xyz": down}),
        ("ws", through.at[1, 0], through.at[1, 1], {"xyz": up}),
        ("wt", through.at[0, 0], through.at[0, 1], {"ta": ta_up}),
        ("rs", back.at[1, 0], back.at[1, 1], {"xyz": down}),
        ("rt", back.at[0, 0], back.at[0, 1], {"ta": ta_down}),
    ):
        i = len(halo)
        halo[name] = pltpu.make_async_remote_copy(
            src, dst, halo_send.at[i], halo_recv.at[i], device_id=to, device_id_type=MESH)
    for name in ("t0", "s1", "t1", "s0"):
        halo[name].start()
    greet(0)
    loads["n0"].wait()
    loads["s11"].wait()
    conjugate_through(1)
    halo["ws"].start()
    loads["n1"].wait()
    loads["t11"].wait()
    conjugate_through(0)
    halo["wt"].start()
    pl.semaphore_wait(met_sem.at[0], 5)
    greet(1)
    packing()
    for name in ("n2", "n3", "n4", "t0"):
        loads[name].wait()
    group("t", 0, 0)
    group("t", 0, 1)
    loads["s00"].wait()
    loads["s10"].wait()
    group("s", 0, 0)
    group("s", 1, 0)
    nil = [jnp.zeros((32, 16), F32)]
    rest = range(ABOVE, 8)
    loads["t10"].wait()
    loads["t11b"].wait()
    loads["s11b"].wait()
    loads["s01"].wait()
    halo["wt"].wait()
    back[0, 0] = merge([blocks_through(0, aw) for aw in range(ABOVE)] + nil * (8 - ABOVE)).astype(BF)
    halo["rt"].start()
    halo["t0"].wait()
    group("t", 1, 0)
    halo["ws"].wait()
    back[1, 0] = merge([blocks_through(1, aw) for aw in range(ABOVE)] + nil * (8 - ABOVE)).astype(BF)
    halo["rs"].start()
    halo["t1"].wait()
    halo["s1"].wait()
    own_t = merge(nil * ABOVE + blocks("t", 1, 1, rest))
    own_s = merge(nil * ABOVE + blocks("s", 1, 1, rest))
    halo["rt"].wait()
    place(0, 3, own_t + back[0, 1].astype(F32))
    pl.semaphore_wait(met_sem.at[1], 3)
    deliver(0)
    halo["s0"].wait()
    group("s", 0, 1)
    halo["rs"].wait()
    place(1, 3, own_s + back[1, 1].astype(F32))
    deliver(1)
    unpacking()
    collect(0)
    collect(1)
    for half in range(2):
        most = send.at[half, pl.ds(0, n_xyz - 1)]
        pltpu.make_async_copy(most, most, row_send.at[half]).wait()


def on_device(nulls, time_links, space_links, owner_lists):
    result = pl.pallas_call(
        kernel,
        out_shape=pltpu.VMEM((64, 1024), BF),
        in_specs=[pl.BlockSpec(memory_space=pl.ANY)] * 3 + [pl.BlockSpec(memory_space=pltpu.VMEM)],
        out_specs=pl.BlockSpec(memory_space=pltpu.VMEM),
        scratch_shapes=[
            pltpu.VMEM((4, 4, 32, 16, 128), BF),
            pltpu.VMEM((2, 4, 32, 64, 128), BF),
            pltpu.VMEM((4, 2, 32, 64, 128), BF),
            pltpu.VMEM((4, 32, 16, 128), BF),
            pltpu.VMEM((4, 32, 16, 128), BF),
            pltpu.VMEM((8, 8, 16, 1024), BF),
            pltpu.VMEM((2, 128, 128), F32),
            pltpu.VMEM((2, 2, 2, 4 * ABOVE, 16, 128), BF),
            pltpu.VMEM((2, 2, 32, 128), BF),
            pltpu.VMEM((32, 256), BF),
            pltpu.VMEM((512, 128), BF),
            pltpu.VMEM((256, 512), BF),
            pltpu.VMEM((2, 32, 16, 128), BF),
            pltpu.VMEM((2, 32, 16, 128), BF),
            pltpu.SemaphoreType.DMA((14,)),
            pltpu.SemaphoreType.DMA((8,)),
            pltpu.SemaphoreType.DMA((8,)),
            pltpu.SemaphoreType.DMA((2,)),
            pltpu.SemaphoreType.DMA((2,)),
            pltpu.SemaphoreType.REGULAR((2,)),
        ],
        compiler_params=pltpu.CompilerParams(collective_id=0, has_side_effects=True),
    )(nulls, time_links, space_links, owner_lists)
    return result.astype(F32)[None]


def solution(mesh):
    return jax.shard_map(
        on_device,
        mesh=mesh,
        in_specs=(
            P("ta", "xyz", None, None, None),
            P("ta", "xyz", None, None, None),
            P("ta", "xyz", None, None, None),
            P(),
        ),
        out_specs=P("ta", "xyz", None),
        check_vma=False,
    )
```

```python
import functools

import jax
import jax.numpy as jnp
from jax import lax
from jax.experimental import pallas as pl
from jax.experimental.pallas import tpu as pltpu
from jax.sharding import PartitionSpec as P

MESH = pl.DeviceIdType.MESH
NY, NZ = 4, 8
ABOVE = 6
BF, F32, I32 = jnp.bfloat16, jnp.float32, jnp.int32


def dot_nt(a, b):
    return lax.dot_general(a, b, (((1,), (1,)), ((), ())), preferred_element_type=F32)


def dot_nn(a, b):
    return lax.dot_general(a, b, (((1,), (0,)), ((), ())), preferred_element_type=F32)


def iota(shape, dim):
    return lax.broadcasted_iota(I32, shape, dim)


def one_hot(cond):
    return jnp.where(cond, 1.0, 0.0).astype(BF)


def swap_halves(x):
    return jnp.concatenate([x[:, 64:], x[:, :64]], axis=1)


def kernel(
    nulls_hbm, tl_hbm, sl_hbm, owner_ref, out_ref,
    nulls, tl, sl, th, sh, held, row_parts, through, back, group_rows, pack, unpack, send, recv,
    link_sem, halo_send, halo_recv, row_send, row_recv, met_sem,
):
    ta = lax.axis_index("ta")
    me = lax.axis_index("xyz")
    n_ta, n_xyz = 8, NY * NZ
    ta_down, ta_up = lax.rem(ta + n_ta - 1, n_ta), lax.rem(ta + 1, n_ta)
    down, up = lax.rem(me + n_xyz - 1, n_xyz), lax.rem(me + 1, n_xyz)
    my_y, my_z = lax.div(me, NZ), lax.rem(me, NZ)
    rows_y = [lax.rem(my_y + dy, NY) * NZ for dy in range(NY)]
    rows_z = [lax.rem(my_z + dz, NZ) for dz in range(NZ)]
    peers = [rows_y[dy] + rows_z[dz] for dz in (4, 3, 5, 2, 6, 1, 7, 0) for dy in (2, 1, 3, 0)][:-1]

    barrier = pltpu.get_barrier_semaphore()
    pl.semaphore_signal(barrier, inc=1, device_id={"ta": ta_down}, device_id_type=MESH)
    pl.semaphore_signal(barrier, inc=1, device_id={"ta": ta_up}, device_id_type=MESH)

    column = [rows_y[dy] + my_z for dy in (2, 1, 3)]
    ring = [rows_y[0] + rows_z[dz] for dz in (2, 6, 1, 7)]
    for peer in [up, down] + ring + column:
        pl.semaphore_signal(barrier, inc=1, device_id={"xyz": peer}, device_id_type=MESH)

    def greet(level):
        for peer in column + (ring[:2] if level == 0 else []):
            pl.semaphore_signal(met_sem.at[level], inc=1, device_id={"xyz": peer}, device_id_type=MESH)

    loads = {}

    def fetch(name, src, dst):
        loads[name] = pltpu.make_async_copy(src, dst, link_sem.at[len(loads)])
        loads[name].start()

    cut = 4 * ABOVE
    early, late = pl.ds(0, cut), pl.ds(cut, 32 - cut)
    low, high = pl.ds(0, 2), pl.ds(2, 2)
    fetch("n0", nulls_hbm.at[high, 3], nulls.at[high, 3])
    fetch("s11", sl_hbm.at[high, 1, early], sl.at[high, 1, early])
    fetch("n1", nulls_hbm.at[3, 2], nulls.at[3, 2])
    fetch("t11", tl_hbm.at[1, high, early], tl.at[1, high, early])
    fetch("n2", nulls_hbm.at[low], nulls.at[low])
    fetch("n3", nulls_hbm.at[high, low], nulls.at[high, low])
    fetch("n4", nulls_hbm.at[2, 2], nulls.at[2, 2])
    fetch("t0", tl_hbm.at[0], tl.at[0])
    fetch("s00", sl_hbm.at[low, 0], sl.at[low, 0])
    fetch("s10", sl_hbm.at[high, 0], sl.at[high, 0])
    fetch("t10", tl_hbm.at[1, low], tl.at[1, low])
    fetch("s01", sl_hbm.at[low, 1], sl.at[low, 1])
    fetch("t11b", tl_hbm.at[1, high, late], tl.at[1, high, late])
    fetch("s11b", sl_hbm.at[high, 1, late], sl.at[high, 1, late])

    def packing():
        row, col = iota((32, 256), 0), iota((32, 256), 1)
        group_rows[...] = one_hot(((row % 8) == (col // 32)) & ((row // 8) == ((col // 8) % 4)))
        lists = owner_ref[...]
        base = me * 32
        place = iota((32, 64), 1)
        first = jnp.sum(jnp.where((lists >= 0) & (lists < base), 1, 0), axis=1, keepdims=True)
        lane = iota((32, 128), 1)
        picks = []
        for r in range(4):
            agg = jnp.sum(jnp.where(place == first + r, lists, 0), axis=1, keepdims=True) - base
            picks.append(one_hot((lane % 32 == agg) & (agg >= 0) & (agg < 32)))
        row, col = iota((512, 128), 0), iota((512, 128), 1)
        spreader = one_hot((row // 16 == col % 32) & (row % 4 == col // 32))
        wide = dot_nn(spreader, jnp.concatenate(picks, axis=0))
        pack[...] = jnp.where((row // 4) % 4 == col // 32, wide, 0.0).astype(BF)

    def unpacking():
        mine = jnp.broadcast_to(owner_ref[pl.ds(me, 1), :], (64, 64))
        r64 = iota((64, 1), 0)
        listed = jnp.sum(jnp.where(iota((64, 64), 1) == r64, mine, 0), axis=1, keepdims=True)
        place = jnp.where(listed >= 0, (listed // 32) * 16 + r64 % 4, -4 * 16)
        col = iota((64, 512), 1)
        for q in range(4):
            unpack[pl.ds(64 * q, 64), :] = one_hot(col == place + 4 * q)

    low16 = iota((16, 128), 1) < 64
    low32 = iota((32, 128), 1) < 64
    turn = jnp.where(low16, 1.0, -1.0).astype(BF)
    spread = one_hot(iota((16, 128), 0) == iota((16, 128), 1) % 16)
    keep = (iota((256, 128), 1) // 16) == (iota((256, 128), 0) % 8)
    none = jnp.zeros((32, 128), BF)

    def images(c, w, links, uppers):
        mats = links(c, w)
        weights = jnp.concatenate(
            [jnp.concatenate([mats[0], mats[2]], axis=0), jnp.concatenate([mats[1], mats[3]], axis=0)], axis=1)
        rows = []
        for i in range(4):
            v = uppers(c, w + i)
            paired = jnp.concatenate([v * turn, swap_halves(v)], axis=0)
            rows.append(jnp.concatenate([none, paired] if i % 2 else [paired, none], axis=1))
        product = dot_nt(jnp.concatenate(rows, axis=0), weights)
        for i in range(2):
            yield jnp.where(low32, product[32 * i:32 * i + 32], product[64 + 32 * i:96 + 32 * i]).astype(BF)

    def conjugates(c, w, lowers):
        for i in range(2):
            a, b = lowers(c, w + i), lowers(c, w + i + 2)
            re = jnp.where(low16, a, swap_halves(b))
            im = jnp.where(low16, swap_halves(a), b)
            yield jnp.concatenate([re, -im], axis=0)
            yield jnp.concatenate([im, re], axis=0)

    def merge(made):
        tiled = dot_nn(jnp.concatenate(made, axis=0).astype(BF), spread)
        return dot_nn(group_rows[...], jnp.where(keep, tiled, 0.0).astype(BF))

    def place(half, part, rows):
        for q in range(4):
            row_parts[half, pl.ds(q * 32 + part * 8, 8), :] = rows[8 * q:8 * q + 8]

    def conjugate_through(half):
        zero = jnp.zeros((16, 128), BF)
        for c in range(2):
            for w in range(0, cut, 4):
                rows = []
                for i in range(4):
                    v = nulls[2 + c, 3, w + i] if half else nulls[3, 2 + c, w + i]
                    t = swap_halves(v)
                    if i % 2 == 0:
                        part = jnp.concatenate([jnp.where(low16, v, zero), jnp.where(low16, t, zero)], axis=0)
                    else:
                        part = jnp.concatenate([jnp.where(low16, zero, t), jnp.where(low16, zero, v)], axis=0)
                    rows.append(jnp.concatenate([part, none] if i < 2 else [none, part], axis=1))
                mats = [sl[2 + c, 1, w + i] if half else tl[1, 2 + c, w + i] for i in range(4)]
                weights = jnp.concatenate(mats, axis=0)
                product = dot_nn(jnp.concatenate(rows, axis=0), weights)
                for i in range(4):
                    top, low = product[32 * i:32 * i + 16], product[32 * i + 16:32 * i + 32]
                    through[half, 0, c, w + i] = (top + jnp.where(low16, swap_halves(low), -swap_halves(low))).astype(BF)

    def blocks_through(half, aw):
        left, right = [], []
        for c in range(2):
            for w in range(4 * aw, 4 * aw + 4):
                v = through[half, 1, c, w]
                left.append(jnp.concatenate([v * turn, swap_halves(v)], axis=0))
                right.append(nulls[2 + c, 0, w] if half else nulls[0, 2 + c, w])
        return dot_nt(jnp.concatenate(left, axis=1), jnp.concatenate(right, axis=1))

    def group(kind, at, ax):
        place(0 if kind == "t" else 1, at * 2 + ax, merge(blocks(kind, at, ax, range(8))))

    def blocks(kind, at, ax, which):
        if kind == "t":
            def links(c, w):
                return [tl[at, 2 * ax + c, w + i] for i in range(4)]

            def uppers(c, w):
                return nulls[2, 2 * ax + c, w] if at == 0 else th[2 * ax + c, w]

            def lowers(c, w):
                return nulls[2 * at + 1, 2 * ax + c, w]
        else:
            def links(c, w):
                return [sl[2 * at + c, ax, w + i] for i in range(4)]

            def uppers(c, w):
                return nulls[2 * at + c, 2, w] if ax == 0 else sh[2 * at + c, w]

            def lowers(c, w):
                return nulls[2 * at + c, 2 * ax + 1, w]
        slot = (at * 2 + ax) + (0 if kind == "t" else 4)
        for aw in which:
            for c in range(2):
                for i, image in enumerate(images(c, 4 * aw, links, uppers)):
                    k = (c * 2 + i) * 256
                    held[slot, aw, :, k:k + 128] = image[:16]
                    held[slot, aw, :, k + 128:k + 256] = image[16:]
        made = []
        for aw in which:
            left = jnp.concatenate([x for c in range(2) for x in conjugates(c, 4 * aw, lowers)], axis=1)
            made.append(dot_nt(left, held[slot, aw]))
        return made

    def deliver(half):
        send[half] = dot_nn(pack[...], row_parts[half].astype(BF)).astype(BF).reshape(n_xyz, 16, 128)
        for peer in peers:
            pltpu.make_async_remote_copy(
                send.at[half, peer], recv.at[half, me], row_send.at[half], row_recv.at[half],
                device_id={"xyz": peer}, device_id_type=MESH).start()
        pltpu.make_async_copy(send.at[half, me], recv.at[half, me], row_recv.at[half]).start()

    def collect(half):
        pltpu.make_async_copy(recv.at[half], recv.at[half], row_recv.at[half]).wait()
        placed = dot_nn(unpack[...], recv[half].reshape(512, 128))
        for q in range(4):
            out_ref[:, half * 512 + q * 128:half * 512 + (q + 1) * 128] = placed[q * 64:(q + 1) * 64].astype(BF)

    packing()
    pl.semaphore_wait(barrier, 11)
    halo = {}
    for name, src, dst, to in (
        ("t0", nulls_hbm.at[0, low], th.at[low], {"ta": ta_down}),
        ("t1", nulls_hbm.at[0, high, late], th.at[high, late], {"ta": ta_down}),
        ("s1", nulls_hbm.at[high, 0, late], sh.at[high, late], {"xyz": down}),
        ("s0", nulls_hbm.at[low, 0], sh.at[low], {"xyz": down}),
        ("ws", through.at[1, 0], through.at[1, 1], {"xyz": up}),
        ("wt", through.at[0, 0], through.at[0, 1], {"ta": ta_up}),
        ("rs", back.at[1, 0], back.at[1, 1], {"xyz": down}),
        ("rt", back.at[0, 0], back.at[0, 1], {"ta": ta_down}),
    ):
        i = len(halo)
        halo[name] = pltpu.make_async_remote_copy(
            src, dst, halo_send.at[i], halo_recv.at[i], device_id=to, device_id_type=MESH)
    for name in ("t0", "s1", "t1", "s0"):
        halo[name].start()
    greet(0)
    loads["n0"].wait()
    loads["s11"].wait()
    conjugate_through(1)
    halo["ws"].start()
    loads["n1"].wait()
    loads["t11"].wait()
    conjugate_through(0)
    halo["wt"].start()
    pl.semaphore_wait(met_sem.at[0], 5)
    greet(1)
    for name in ("n2", "n3", "n4", "t0"):
        loads[name].wait()
    group("t", 0, 0)
    group("t", 0, 1)
    loads["s00"].wait()
    loads["s10"].wait()
    group("s", 0, 0)
    group("s", 1, 0)
    nil = [jnp.zeros((32, 16), F32)]
    rest = range(ABOVE, 8)
    loads["t10"].wait()
    loads["t11b"].wait()
    loads["s11b"].wait()
    loads["s01"].wait()
    halo["wt"].wait()
    back[0, 0] = merge([blocks_through(0, aw) for aw in range(ABOVE)] + nil * (8 - ABOVE)).astype(BF)
    halo["rt"].start()
    halo["t0"].wait()
    group("t", 1, 0)
    halo["ws"].wait()
    back[1, 0] = merge([blocks_through(1, aw) for aw in range(ABOVE)] + nil * (8 - ABOVE)).astype(BF)
    halo["rs"].start()
    halo["t1"].wait()
    halo["s1"].wait()
    own_t = merge(nil * ABOVE + blocks("t", 1, 1, rest))
    own_s = merge(nil * ABOVE + blocks("s", 1, 1, rest))
    halo["rt"].wait()
    place(0, 3, own_t + back[0, 1].astype(F32))
    pl.semaphore_wait(met_sem.at[1], 3)
    deliver(0)
    halo["s0"].wait()
    group("s", 0, 1)
    halo["rs"].wait()
    place(1, 3, own_s + back[1, 1].astype(F32))
    deliver(1)
    unpacking()
    collect(0)
    collect(1)
    for half in range(2):
        most = send.at[half, pl.ds(0, n_xyz - 1)]
        pltpu.make_async_copy(most, most, row_send.at[half]).wait()


def on_device(nulls, time_links, space_links, owner_lists):
    result = pl.pallas_call(
        kernel,
        out_shape=pltpu.VMEM((64, 1024), BF),
        in_specs=[pl.BlockSpec(memory_space=pl.ANY)] * 3 + [pl.BlockSpec(memory_space=pltpu.VMEM)],
        out_specs=pl.BlockSpec(memory_space=pltpu.VMEM),
        scratch_shapes=[
            pltpu.VMEM((4, 4, 32, 16, 128), BF),
            pltpu.VMEM((2, 4, 32, 64, 128), BF),
            pltpu.VMEM((4, 2, 32, 64, 128), BF),
            pltpu.VMEM((4, 32, 16, 128), BF),
            pltpu.VMEM((4, 32, 16, 128), BF),
            pltpu.VMEM((8, 8, 16, 1024), BF),
            pltpu.VMEM((2, 128, 128), F32),
            pltpu.VMEM((2, 2, 2, 4 * ABOVE, 16, 128), BF),
            pltpu.VMEM((2, 2, 32, 128), BF),
            pltpu.VMEM((32, 256), BF),
            pltpu.VMEM((512, 128), BF),
            pltpu.VMEM((256, 512), BF),
            pltpu.VMEM((2, 32, 16, 128), BF),
            pltpu.VMEM((2, 32, 16, 128), BF),
            pltpu.SemaphoreType.DMA((14,)),
            pltpu.SemaphoreType.DMA((8,)),
            pltpu.SemaphoreType.DMA((8,)),
            pltpu.SemaphoreType.DMA((2,)),
            pltpu.SemaphoreType.DMA((2,)),
            pltpu.SemaphoreType.REGULAR((2,)),
        ],
        compiler_params=pltpu.CompilerParams(collective_id=0, has_side_effects=True),
    )(nulls, time_links, space_links, owner_lists)
    return result.astype(F32)[None]


def solution(mesh):
    return jax.shard_map(
        on_device,
        mesh=mesh,
        in_specs=(
            P("ta", "xyz", None, None, None),
            P("ta", "xyz", None, None, None),
            P("ta", "xyz", None, None, None),
            P(),
        ),
        out_specs=P("ta", "xyz", None),
        check_vma=False,
    )
```
